256 devices in a mesh: rows: 64 (over z, y, core), rhs: 4 (over x).
Axes of the slice: x: 4, y: 4, z: 8, core: 2. Of those that a mesh axis runs over, the one named last changes fastest.
Arguments:
- right_sides: bfloat16 [64, 131072], P('rhs', 'rows'), may hold values from -6 to 6
- lower_inverse: bfloat16 [512, 256, 256], P('rows'), may hold values from -0.375 to 0.375
- lower_left: bfloat16 [512, 256, 32], P('rows'), may hold values from -1 to 1
- lower_right: bfloat16 [512, 256, 32], P('rows'), may hold values from -0.005859375 to 0.005859375
- upper_inverse: bfloat16 [512, 256, 256], P('rows'), may hold values from -0.375 to 0.375
- upper_left: bfloat16 [512, 256, 32], P('rows'), may hold values from -1 to 1
- upper_right: bfloat16 [512, 256, 32], P('rows'), may hold values from -0.005859375 to 0.005859375
- block_ranks: int32 [2, 512], P(None, 'rows'), may hold values from 8 to 32
Outputs:
- first_solve: float32 [64, 131072], P('rhs', 'rows')
- second_solve: float32 [64, 131072], P('rhs', 'rows')
The draws below stay inside these ranges and needn't reach their ends.
All inputs are finite; a program needn't handle non-finite values.
Results may differ from the reference program's by a relative error of at most 0.0051.
Values may be sent and summed in bfloat16 or wider, within the bound.
No kernel may reach another device: no remote copies, remote signals or barrier semaphores. Data moves between devices by JAX's collectives and lax.ppermute only.
A program may use at most 64 MiB of HBM per device.

```python
import jax
import jax.numpy as jnp
from jax import lax

BS = 256
RANK = 32
RHS = 64
NBLK = 512
ORDER = 131072


def with_ends(drawn, own_key, low, largest):
    place = [jax.random.randint(jax.random.fold_in(own_key, axis), (), 0, length) for axis, length in enumerate(drawn.shape)]
    main_axis = drawn.shape.index(max(drawn.shape))
    beside = place[:main_axis] + [(place[main_axis] + 1) % drawn.shape[main_axis]] + place[main_axis + 1:]
    return drawn.at[tuple(place)].set(low).at[tuple(beside)].set(largest)


def levels(rng, extent, shards, least, high):
    gain = 1.0
    for position, shards_of in shards:
        heights = jax.random.uniform(jax.random.fold_in(jax.random.fold_in(rng, 6), position), (shards_of,), jnp.float32, least / len(shards), high / len(shards))
        gain = gain * jnp.repeat(jnp.exp(heights), extent[position] // shards_of).reshape((-1,) + (1,) * (len(extent) - 1 - position))
    return gain


def bell_draw(own_key, shape, deviation, bound, pieces=(), kind=jnp.bfloat16):
    entries = jax.random.normal(own_key, shape, jnp.float32) * deviation
    if len(pieces) > 0:
        entries = levels(own_key, shape, pieces, -0.22, 0.18) * entries
    return jnp.clip(entries, min=-bound, max=bound).astype(kind)


def setup_inputs(seed: int = 0) -> dict:
    arg_keys = jax.random.split(jax.random.key(seed), 9)
    right_sides = bell_draw(arg_keys[0], (RHS, ORDER), 1.0, 6.0, ((0, 4), (1, 64)))
    lower_inverse = bell_draw(arg_keys[1], (NBLK, BS, BS), BS ** -0.5, 0.375, ((0, 64),))
    lower_left = bell_draw(arg_keys[2], (NBLK, BS, RANK), RANK ** -0.5, 1.0, ((0, 64),))
    lower_right = bell_draw(arg_keys[3], (NBLK, BS, RANK), (8 * NBLK * BS) ** -0.5, 0.005859375, ((0, 64),))
    upper_inverse = bell_draw(arg_keys[4], (NBLK, BS, BS), BS ** -0.5, 0.375, ((0, 64),))
    upper_left = bell_draw(arg_keys[5], (NBLK, BS, RANK), RANK ** -0.5, 1.0, ((0, 64),))
    upper_right = bell_draw(arg_keys[6], (NBLK, BS, RANK), (8 * NBLK * BS) ** -0.5, 0.005859375, ((0, 64),))
    block_ranks = with_ends(jax.random.randint(arg_keys[7], (2, NBLK), RANK // 4, RANK + 1), jax.random.fold_in(arg_keys[7], 1), RANK // 4, RANK).astype(jnp.int32)
    return {"right_sides": right_sides, "lower_inverse": lower_inverse, "lower_left": lower_left, "lower_right": lower_right, "upper_inverse": upper_inverse, "upper_left": upper_left, "upper_right": upper_right, "block_ranks": block_ranks}


highest = lax.Precision.HIGHEST


def factors(inverse, left_factor, right_factor, ranks_row):
    product = jnp.einsum("bij,bjk->bik", inverse.astype(jnp.float32), left_factor.astype(jnp.float32))
    rounded = lax.optimization_barrier(product.astype(jnp.bfloat16))
    coupled = rounded.astype(jnp.float32)
    columns = jnp.arange(RANK, dtype=jnp.int32)
    rank_mask = (columns[None, :] < ranks_row[:, None]).astype(jnp.float32)
    masked = right_factor.astype(jnp.float32) * rank_mask[:, None, :]
    return coupled, masked


def sweep_blocks(values, inverse, coupled, masked, reverse):
    blocked = values.reshape(RHS, NBLK, BS).astype(jnp.float32)
    pushed = jnp.einsum("rbk,bjk->brj", blocked, inverse.astype(jnp.float32))

    def advance(state, inputs):
        pushed_row, coupled_row, masked_row = inputs
        solved = pushed_row - jnp.dot(state, coupled_row.T, precision=highest)
        state = state + jnp.dot(solved, masked_row, precision=highest)
        return state, solved

    start = jnp.zeros((RHS, RANK), jnp.float32)
    _, solved = lax.scan(advance, start, (pushed, coupled, masked), reverse=reverse)
    return jnp.transpose(solved, (1, 0, 2)).reshape(RHS, NBLK * BS)


def reference(right_sides, lower_inverse, lower_left, lower_right, upper_inverse, upper_left, upper_right, block_ranks):
    lower_coupled, lower_masked = factors(lower_inverse, lower_left, lower_right, block_ranks[0])
    upper_coupled, upper_masked = factors(upper_inverse, upper_left, upper_right, block_ranks[1])
    forward = sweep_blocks(right_sides, lower_inverse, lower_coupled, lower_masked, False)
    first_solve = sweep_blocks(forward.astype(jnp.bfloat16), upper_inverse, upper_coupled, upper_masked, True)
    forward_again = sweep_blocks(first_solve.astype(jnp.bfloat16), lower_inverse, lower_coupled, lower_masked, False)
    second_solve = sweep_blocks(forward_again.astype(jnp.bfloat16), upper_inverse, upper_coupled, upper_masked, True)
    return first_solve, second_solve
```

```python
import functools

import jax
import jax.numpy as jnp
from jax import lax
from jax.experimental import pallas as pl
from jax.experimental.pallas import tpu as pltpu
from jax.sharding import PartitionSpec as P

f32, bf16 = jnp.float32, jnp.bfloat16

BS = 256
RANK = 32
RHS = 16
FAN = 8
WIDE = FAN * RANK
ROWS = RHS + 2 * RANK


def roll(x, shift):
    shift %= x.shape[1]
    return pltpu.roll(x, shift, 1) if shift else x


def split(x):
    high = x.astype(bf16)
    return high, (x - high.astype(f32)).astype(bf16)


def dot_nn(x, w):
    return lax.dot_general(x, w, (((1,), (0,)), ((), ())), preferred_element_type=f32)


def dot_nt(x, w):
    return lax.dot_general(x, w, (((1,), (1,)), ((), ())), preferred_element_type=f32)


def wide_times_exact(x, w, dot):
    n = x.shape[0]
    both = dot(jnp.concatenate(split(x), axis=0), w)
    return both[:n] + both[n:]


def times(x, w):
    n = x.shape[0]
    high, low = split(x)
    both = dot_nn(jnp.concatenate([high, low], axis=0), w[0])
    return both[:n] + both[n:] + dot_nn(high, w[1])


def block_ids(shape):
    return (
        lax.broadcasted_iota(jnp.int32, shape, 0) // RANK,
        lax.broadcasted_iota(jnp.int32, shape, 1) // RANK,
    )


def placed(tiled, offset):
    row, col = block_ids(tiled.shape)
    return jnp.where(col == row + offset, tiled, 0.0)


def carries(tiled, step):
    row, col = block_ids((WIDE, WIDE))
    one = (
        lax.broadcasted_iota(jnp.int32, (WIDE, WIDE), 0)
        == lax.broadcasted_iota(jnp.int32, (WIDE, WIDE), 1)
    ).astype(f32)
    hop = placed(tiled, step)
    hop_parts = split(hop)
    two = times(hop, hop_parts)
    two_parts = split(two)
    three = times(hop, two_parts)
    four = times(two, two_parts)
    near = one + hop + two + three
    return near + times(near, split(four))


def sweeps(offsets, maps, outward):
    o1, o2, o3, o4 = offsets
    t, r, a21, a31, a32, a41, a42 = maps
    up = carries(t, 1)
    down = carries(r, -1)
    gap = jnp.zeros((RANK, WIDE), f32)
    up_next = split(jnp.concatenate([up[RANK:], gap], axis=0))
    down_next = split(jnp.concatenate([gap, down[:-RANK]], axis=0))
    d21, d31, d32, d41, d42 = (split(placed(a, 0)) for a in (a21, a31, a32, a41, a42))

    def with_rows(x, rows):
        if not outward:
            return x
        return jnp.concatenate([x, jnp.zeros((rows - x.shape[0], WIDE), f32)], axis=0)

    e1 = times(o1, up_next)
    if outward:
        e1 = jnp.concatenate([e1, up[:RANK]], axis=0)
    q2 = with_rows(o2, RHS + RANK) + times(e1, d21)
    e2 = times(q2, down_next)
    if outward:
        e2 = jnp.concatenate([e2, down[-RANK:]], axis=0)
    q3 = with_rows(o3, ROWS) + with_rows(times(e1, d31), ROWS) + times(e2, d32)
    e3 = times(q3, up_next)
    q4 = with_rows(o4, ROWS) + with_rows(times(e1, d41), ROWS) + times(e2, d42) + times(e3, d21)
    e4 = times(q4, down_next)
    entering = (e1, e2, e3, e4)
    if not outward:
        return entering, None
    dt, dr = split(placed(t, 0)), split(placed(r, 0))
    last, first = slice(128, 256), slice(0, 128)
    group = lax.broadcasted_iota(jnp.int32, (ROWS, 128), 1) // RANK
    t1 = roll(with_rows(with_rows(o1, RHS + RANK) + times(e1, dt), ROWS)[:, last], 32)
    t2 = roll((with_rows(q2, ROWS) + times(e2, dr))[:, first], 32)
    t3 = roll((q3 + times(e3, dt))[:, last], 96)
    t4 = roll((q4 + times(e4, dr))[:, first], 96)
    packed = jnp.where(
        group == 0, t1, jnp.where(group == 1, t2, jnp.where(group == 2, t3, t4))
    )
    return entering, packed


def unpack(received):
    own = received[:, RHS : RHS + RANK].reshape(WIDE, 128)
    cross = received[:, RHS + RANK :].reshape(WIDE, 128)
    lane_group = lax.broadcasted_iota(jnp.int32, (WIDE, 128), 1) // RANK

    def tiled(x, group):
        x = jnp.where(lane_group == group, x, 0.0)
        x = x + roll(x, 32)
        x = x + roll(x, 64)
        return jnp.concatenate([x, x], axis=1)

    maps = (
        tiled(own, 0),
        tiled(cross, 1),
        tiled(own, 1),
        tiled(own, 2),
        tiled(cross, 2),
        tiled(own, 3),
        tiled(cross, 3),
    )
    group = lax.broadcasted_iota(jnp.int32, (RHS, 128), 1) // RANK
    offsets = []
    for k in range(4):
        halves = []
        for half in range(2):
            out = jnp.zeros((RHS, 128), f32)
            for g in range(4):
                moved = roll(received[4 * half + g, :RHS], 32 * (g - k))
                out = jnp.where(group == g, moved, out)
            halves.append(out)
        offsets.append(jnp.concatenate(halves, axis=1))
    return tuple(offsets), maps


def own_piece(entering, piece):
    rows = entering[-1].shape[0]
    col = lax.broadcasted_iota(jnp.int32, (rows, WIDE), 1) // RANK
    group = lax.broadcasted_iota(jnp.int32, (rows, 128), 1) // RANK
    out = jnp.zeros((rows, 128), f32)
    for k, e in enumerate(entering):
        if e.shape[0] < rows:
            e = jnp.concatenate([e, jnp.zeros((rows - e.shape[0], WIDE), f32)], axis=0)
        e = jnp.where(col == piece, e, 0.0)
        e = e[:, :128] + e[:, 128:]
        e = e + roll(e, 32)
        e = e + roll(e, 64)
        out = jnp.where(group == k, e, out)
    return out


def moved_on(x):
    return jnp.where(lax.broadcasted_iota(jnp.int32, x.shape, 1) >= 64, roll(x, 64), 0.0)


def pieces_kernel(
    ranks, v, li, ll, lr, ui, ul, ur, packed_out, e1_out, e2_out, e3_out, e4_out, rows_out, data_out
):
    lane = lax.broadcasted_iota(jnp.int32, (BS, WIDE), 1)
    col = lax.broadcasted_iota(jnp.int32, (RHS, WIDE), 1) // RANK
    eye = (
        lax.broadcasted_iota(jnp.int32, (RANK, WIDE), 0)
        == lax.broadcasted_iota(jnp.int32, (RANK, WIDE), 1) % RANK
    ).astype(f32)
    offsets = [jnp.zeros((RHS, WIDE), f32) for _ in range(4)]
    maps = [[] for _ in range(7)]
    for i in range(FAN):
        a, b = li[i], ui[i]
        vi = v[:, BS * i : BS * (i + 1)]
        left_a = ll[i].astype(f32).T.astype(bf16)
        left_b = ul[i].astype(f32).T.astype(bf16)

        def masked(right, factor):
            w = right[i].astype(f32)
            w = jnp.concatenate([w] * FAN, axis=1)
            return jnp.where(lane % RANK < ranks[factor, i], w, 0.0).astype(bf16)

        m, n = masked(lr, 0), masked(ur, 1)
        one = dot_nt(jnp.concatenate([vi, left_a], axis=0), a)
        va = one[:RHS]
        c = (-one[RHS:]).astype(bf16)
        d = (-dot_nt(left_b, b)).astype(bf16)
        va_parts = split(va)
        two = dot_nt(jnp.concatenate([va_parts[0], va_parts[1], c], axis=0), b)
        vab = two[:RHS] + two[RHS : 2 * RHS]
        cb = two[2 * RHS :]
        both = split(jnp.concatenate([vab, cb], axis=0))
        three = dot_nt(jnp.concatenate([both[0], both[1], d], axis=0), a)
        k = RHS + RANK
        vaba_cba = three[:k] + three[k : 2 * k]
        da = three[2 * k :]
        last = jnp.concatenate([vaba_cba, da], axis=0)
        four = wide_times_exact(last, b, dot_nt)
        lo_parts = split(jnp.concatenate([va, last], axis=0))
        lo_n = lo_parts[0].shape[0]
        low = dot_nn(jnp.concatenate([lo_parts[0], lo_parts[1], c], axis=0), m)
        lo = low[:lo_n] + low[lo_n : 2 * lo_n]
        cm = low[2 * lo_n :]
        hi_parts = split(jnp.concatenate([vab, cb, four], axis=0))
        hi_n = hi_parts[0].shape[0]
        high = dot_nn(jnp.concatenate([hi_parts[0], hi_parts[1], d], axis=0), n)
        hi = high[:hi_n] + high[hi_n : 2 * hi_n]
        dn = high[2 * hi_n :]
        o = (lo[:RHS], hi[:RHS], lo[RHS : 2 * RHS], hi[k : k + RHS])
        for j in range(4):
            offsets[j] = jnp.where(col == i, o[j], offsets[j])
        maps[0].append(eye + cm)
        maps[1].append(eye + dn)
        maps[2].append(hi[RHS:k])
        maps[3].append(lo[2 * RHS : 2 * RHS + RANK])
        maps[4].append(lo[2 * RHS + RANK :])
        maps[5].append(hi[k + RHS : k + RHS + RANK])
        maps[6].append(hi[k + RHS + RANK :])
        span = slice(BS * i, BS * (i + 1))
        rows_out[:, span] = jnp.concatenate(
            [four[RHS:], cb, d.astype(f32)], axis=0
        )
        data_out[:, span] = jnp.concatenate([vab, four[:RHS]], axis=0)
    maps = [jnp.concatenate(m, axis=0) for m in maps]
    entering, packed = sweeps(offsets, maps, True)
    for e in range(FAN):
        packed_out[e] = packed
    e1, e2, e3, e4 = entering
    e1_out[...] = jnp.concatenate([e1, jnp.zeros((RANK, WIDE), f32)], axis=0)
    e2_out[...] = e2
    e3_out[...] = e3
    e4_out[...] = e4


def response_kernel(e1, e2, e3, e4, rows, data, high_out, low_out, base_out):
    entering = (e1[...], e2[...], e3[...], e4[...])
    for i in range(FAN):
        span = slice(BS * i, BS * (i + 1))
        s = own_piece(entering, i)
        both = jnp.concatenate([s, moved_on(s)], axis=0)
        y = times(both, split(rows[:, span]))
        base_out[:, span] = data[:, span] + jnp.concatenate(
            [y[ROWS : ROWS + RHS], y[:RHS]], axis=0
        )
        gain = split(jnp.concatenate([y[RHS:ROWS], y[ROWS + RHS :]], axis=0))
        high_out[:, span] = gain[0]
        low_out[:, span] = gain[1]


def plane_kernel(place, received, packed_out, own_out):
    offsets, maps = unpack(received[...])
    entering, packed = sweeps(offsets, maps, True)
    for e in range(FAN):
        packed_out[e] = packed
    own_out[...] = own_piece(entering, place[0])


def outputs_kernel(place, received, own, high, low, base, first_out, second_out):
    offsets, maps = unpack(received[...])
    entering, _ = sweeps(offsets, maps, False)
    plane = own_piece(entering, place[1])
    mine = own[...]
    s1, s2 = mine[RHS : RHS + RANK], mine[RHS + RANK :]
    gain = jnp.concatenate([s1, s2, moved_on(s1), moved_on(s2)], axis=0)
    state = mine[:RHS] + times(plane, split(gain))
    both = jnp.concatenate([moved_on(state), state], axis=0)
    y = base[...] + times(both, (high[...], low[...]))
    first_out[...] = y[:RHS]
    second_out[...] = y[RHS:]


vmem = pl.BlockSpec(memory_space=pltpu.VMEM)
smem = pl.BlockSpec(memory_space=pltpu.SMEM)


def call(kernel, name, out, n_smem, *args):
    return pl.pallas_call(
        kernel,
        out_shape=out,
        in_specs=[smem] * n_smem + [vmem] * (len(args) - n_smem),
        out_specs=jax.tree.map(lambda _: vmem, out),
        compiler_params=pltpu.CompilerParams(vmem_limit_bytes=48 << 20),
        name=name,
    )(*args)


def shape(*dims, dtype=f32):
    return jax.ShapeDtypeStruct(dims, dtype)


def local(
    right_sides, lower_inverse, lower_left, lower_right, upper_inverse, upper_left, upper_right, block_ranks
):
    order = right_sides.shape[1]
    index = lax.axis_index("rows")
    place = jnp.stack([index % FAN, index // FAN]).astype(jnp.int32)
    in_plane = [[p * FAN + d for d in range(FAN)] for p in range(FAN)]
    across = [[p * FAN + d for p in range(FAN)] for d in range(FAN)]
    state = shape(ROWS, WIDE)
    packed, e1, e2, e3, e4, rows, data = call(
        pieces_kernel,
        "pieces",
        (shape(FAN, ROWS, 128), state, state, state, state, shape(4 * RANK, order), shape(2 * RHS, order)),
        1,
        block_ranks,
        right_sides,
        lower_inverse,
        lower_left,
        lower_right,
        upper_inverse,
        upper_left,
        upper_right,
    )
    received = lax.all_to_all(packed, "rows", 0, 0, tiled=True, axis_index_groups=in_plane)
    high, low, base = call(
        response_kernel,
        "response",
        (shape(4 * RANK, order, dtype=bf16), shape(4 * RANK, order, dtype=bf16), shape(2 * RHS, order)),
        0,
        e1,
        e2,
        e3,
        e4,
        rows,
        data,
    )
    packed, own = call(
        plane_kernel, "plane", (shape(FAN, ROWS, 128), shape(ROWS, 128)), 1, place, received
    )
    received = lax.all_to_all(packed, "rows", 0, 0, tiled=True, axis_index_groups=across)
    return call(
        outputs_kernel,
        "outputs",
        (shape(RHS, order), shape(RHS, order)),
        1,
        place,
        received,
        own,
        high,
        low,
        base,
    )


def solution(mesh):
    placed_in = (
        P("rhs", "rows"),
        P("rows", None, None),
        P("rows", None, None),
        P("rows", None, None),
        P("rows", None, None),
        P("rows", None, None),
        P("rows", None, None),
        P(None, "rows"),
    )
    return jax.shard_map(
        local,
        mesh=mesh,
        in_specs=placed_in,
        out_specs=(P("rhs", "rows"), P("rhs", "rows")),
        check_vma=False,
    )
```

```python
import functools

import jax
import jax.numpy as jnp
from jax import lax
from jax.experimental import pallas as pl
from jax.experimental.pallas import tpu as pltpu
from jax.sharding import PartitionSpec as P

f32, bf16 = jnp.float32, jnp.bfloat16

BS = 256
RANK = 32
RHS = 16
FAN = 8
WIDE = FAN * RANK
ROWS = RHS + 2 * RANK


def roll(x, shift):
    shift %= x.shape[1]
    return pltpu.roll(x, shift, 1) if shift else x


def split(x):
    high = x.astype(bf16)
    return high, (x - high.astype(f32)).astype(bf16)


def dot_nn(x, w):
    return lax.dot_general(x, w, (((1,), (0,)), ((), ())), preferred_element_type=f32)


def dot_nt(x, w):
    return lax.dot_general(x, w, (((1,), (1,)), ((), ())), preferred_element_type=f32)


def wide_times_exact(x, w, dot):
    n = x.shape[0]
    both = dot(jnp.concatenate(split(x), axis=0), w)
    return both[:n] + both[n:]


def times(x, w):
    n = x.shape[0]
    high, low = split(x)
    both = dot_nn(jnp.concatenate([high, low], axis=0), w[0])
    return both[:n] + both[n:] + dot_nn(high, w[1])


def block_ids(shape):
    return (
        lax.broadcasted_iota(jnp.int32, shape, 0) // RANK,
        lax.broadcasted_iota(jnp.int32, shape, 1) // RANK,
    )


def placed(tiled, offset):
    row, col = block_ids(tiled.shape)
    return jnp.where(col == row + offset, tiled, 0.0)


def carries(tiled, step):
    row, col = block_ids((WIDE, WIDE))
    one = (
        lax.broadcasted_iota(jnp.int32, (WIDE, WIDE), 0)
        == lax.broadcasted_iota(jnp.int32, (WIDE, WIDE), 1)
    ).astype(f32)
    hop = placed(tiled, step)
    hop_parts = split(hop)
    two = times(hop, hop_parts)
    two_parts = split(two)
    three = times(hop, two_parts)
    four = times(two, two_parts)
    near = one + hop + two + three
    return near + times(near, split(four))


def sweeps(offsets, maps, outward):
    o1, o2, o3, o4 = offsets
    t, r, a21, a31, a32, a41, a42 = maps
    up = carries(t, 1)
    down = carries(r, -1)
    gap = jnp.zeros((RANK, WIDE), f32)
    up_next = split(jnp.concatenate([up[RANK:], gap], axis=0))
    down_next = split(jnp.concatenate([gap, down[:-RANK]], axis=0))
    d21, d31, d32, d41, d42 = (split(placed(a, 0)) for a in (a21, a31, a32, a41, a42))

    def with_rows(x, rows):
        if not outward:
            return x
        return jnp.concatenate([x, jnp.zeros((rows - x.shape[0], WIDE), f32)], axis=0)

    e1 = times(o1, up_next)
    if outward:
        e1 = jnp.concatenate([e1, up[:RANK]], axis=0)
    q2 = with_rows(o2, RHS + RANK) + times(e1, d21)
    e2 = times(q2, down_next)
    if outward:
        e2 = jnp.concatenate([e2, down[-RANK:]], axis=0)
    q3 = with_rows(o3, ROWS) + with_rows(times(e1, d31), ROWS) + times(e2, d32)
    e3 = times(q3, up_next)
    q4 = with_rows(o4, ROWS) + with_rows(times(e1, d41), ROWS) + times(e2, d42) + times(e3, d21)
    e4 = times(q4, down_next)
    entering = (e1, e2, e3, e4)
    if not outward:
        return entering, None
    dt, dr = split(placed(t, 0)), split(placed(r, 0))
    last, first = slice(128, 256), slice(0, 128)
    group = lax.broadcasted_iota(jnp.int32, (ROWS, 128), 1) // RANK
    t1 = roll(with_rows(with_rows(o1, RHS + RANK) + times(e1, dt), ROWS)[:, last], 32)
    t2 = roll((with_rows(q2, ROWS) + times(e2, dr))[:, first], 32)
    t3 = roll((q3 + times(e3, dt))[:, last], 96)
    t4 = roll((q4 + times(e4, dr))[:, first], 96)
    packed = jnp.where(
        group == 0, t1, jnp.where(group == 1, t2, jnp.where(group == 2, t3, t4))
    )
    return entering, packed


def unpack(received):
    own = received[:, RHS : RHS + RANK].reshape(WIDE, 128)
    cross = received[:, RHS + RANK :].reshape(WIDE, 128)
    lane_group = lax.broadcasted_iota(jnp.int32, (WIDE, 128), 1) // RANK

    def tiled(x, group):
        x = jnp.where(lane_group == group, x, 0.0)
        x = x + roll(x, 32)
        x = x + roll(x, 64)
        return jnp.concatenate([x, x], axis=1)

    maps = (
        tiled(own, 0),
        tiled(cross, 1),
        tiled(own, 1),
        tiled(own, 2),
        tiled(cross, 2),
        tiled(own, 3),
        tiled(cross, 3),
    )
    group = lax.broadcasted_iota(jnp.int32, (RHS, 128), 1) // RANK
    offsets = []
    for k in range(4):
        halves = []
        for half in range(2):
            out = jnp.zeros((RHS, 128), f32)
            for g in range(4):
                moved = roll(received[4 * half + g, :RHS], 32 * (g - k))
                out = jnp.where(group == g, moved, out)
            halves.append(out)
        offsets.append(jnp.concatenate(halves, axis=1))
    return tuple(offsets), maps


def own_piece(entering, piece):
    rows = entering[-1].shape[0]
    col = lax.broadcasted_iota(jnp.int32, (rows, WIDE), 1) // RANK
    group = lax.broadcasted_iota(jnp.int32, (rows, 128), 1) // RANK
    out = jnp.zeros((rows, 128), f32)
    for k, e in enumerate(entering):
        if e.shape[0] < rows:
            e = jnp.concatenate([e, jnp.zeros((rows - e.shape[0], WIDE), f32)], axis=0)
        e = jnp.where(col == piece, e, 0.0)
        e = e[:, :128] + e[:, 128:]
        e = e + roll(e, 32)
        e = e + roll(e, 64)
        out = jnp.where(group == k, e, out)
    return out


def moved_on(x):
    return jnp.where(lax.broadcasted_iota(jnp.int32, x.shape, 1) >= 64, roll(x, 64), 0.0)


def pieces_kernel(
    ranks_any, v_any, li_any, ll_any, lr_any, ui_any, ul_any, ur_any,
    packed_out, entering_out, rows_out, data_out,
    ranks, v, li, ll, lr, ui, ul, ur, sems,
):
    copies = {}

    def start(name, source, target, at):
        copies[name] = pltpu.make_async_copy(source, target, sems.at[at])
        copies[name].start()

    start("v", v_any, v, 0)
    start("ll", ll_any, ll, 1)
    for i in range(FAN):
        start(("a", i), li_any.at[i], li.at[i], 6 + i)
    start("ul", ul_any, ul, 2)
    for i in range(FAN):
        start(("b", i), ui_any.at[i], ui.at[i], 6 + FAN + i)
    start("lr", lr_any, lr, 3)
    start("ur", ur_any, ur, 4)
    start("ranks", ranks_any, ranks, 5)

    col = lax.broadcasted_iota(jnp.int32, (RHS, WIDE), 1) // RANK
    eye = (
        lax.broadcasted_iota(jnp.int32, (RANK, WIDE), 0)
        == lax.broadcasted_iota(jnp.int32, (RANK, WIDE), 1) % RANK
    ).astype(f32)
    blocks = range(FAN)
    span = [slice(BS * i, BS * (i + 1)) for i in blocks]
    k = RHS + RANK
    va, c, d, vab, cb, last, four = ([None] * FAN for _ in range(7))
    copies["v"].wait()
    copies["ll"].wait()
    for i in blocks:
        copies["a", i].wait()
        one = dot_nt(jnp.concatenate([v[:, span[i]], ll[i]], axis=0), li[i])
        va[i] = one[:RHS]
        c[i] = (-one[RHS:]).astype(bf16)
    copies["ul"].wait()
    for i in blocks:
        copies["b", i].wait()
        two = dot_nt(jnp.concatenate([*split(va[i]), c[i], ul[i]], axis=0), ui[i])
        vab[i] = two[:RHS] + two[RHS : 2 * RHS]
        cb[i] = two[2 * RHS : 2 * RHS + RANK]
        d[i] = (-two[2 * RHS + RANK :]).astype(bf16)
    for i in blocks:
        both = split(jnp.concatenate([vab[i], cb[i]], axis=0))
        three = dot_nt(jnp.concatenate([*both, d[i]], axis=0), li[i])
        last[i] = jnp.concatenate([three[:k] + three[k : 2 * k], three[2 * k :]], axis=0)
    for i in blocks:
        four[i] = wide_times_exact(last[i], ui[i], dot_nt)
        rows_out[:, span[i]] = jnp.concatenate([four[i][RHS:], cb[i], d[i].astype(f32)], axis=0)
        data_out[:, span[i]] = jnp.concatenate([vab[i], four[i][:RHS]], axis=0)
    copies["lr"].wait()
    copies["ur"].wait()
    copies["ranks"].wait()

    def masked(right, rank):
        keep = lax.broadcasted_iota(jnp.int32, (RANK, BS), 0) < rank
        w = jnp.where(keep, right.astype(f32), 0.0).astype(bf16)
        return jnp.concatenate([w] * FAN, axis=0)

    offsets = [jnp.zeros((RHS, WIDE), f32) for _ in range(4)]
    maps = [[] for _ in range(7)]
    for i in blocks:
        m, n = masked(lr[i], ranks[0, i]), masked(ur[i], ranks[1, i])
        parts = split(jnp.concatenate([va[i], last[i]], axis=0))
        rows = parts[0].shape[0]
        low = dot_nt(jnp.concatenate([*parts, c[i]], axis=0), m)
        lo, cm = low[:rows] + low[rows : 2 * rows], low[2 * rows :]
        parts = split(jnp.concatenate([vab[i], cb[i], four[i]], axis=0))
        rows = parts[0].shape[0]
        high = dot_nt(jnp.concatenate([*parts, d[i]], axis=0), n)
        hi, dn = high[:rows] + high[rows : 2 * rows], high[2 * rows :]
        o = (lo[:RHS], hi[:RHS], lo[RHS : 2 * RHS], hi[k : k + RHS])
        for j in range(4):
            offsets[j] = jnp.where(col == i, o[j], offsets[j])
        maps[0].append(eye + cm)
        maps[1].append(eye + dn)
        maps[2].append(hi[RHS:k])
        maps[3].append(lo[2 * RHS : 2 * RHS + RANK])
        maps[4].append(lo[2 * RHS + RANK :])
        maps[5].append(hi[k + RHS : k + RHS + RANK])
        maps[6].append(hi[k + RHS + RANK :])
    maps = [jnp.concatenate(m, axis=0) for m in maps]
    entering, packed = sweeps(offsets, maps, True)
    packed_out[...] = packed
    for j, e in enumerate(entering):
        entering_out[j, : e.shape[0]] = e
        if e.shape[0] < ROWS:
            entering_out[j, e.shape[0] :] = jnp.zeros((ROWS - e.shape[0], WIDE), f32)


def device_gain(own):
    s1, s2 = own[RHS : RHS + RANK], own[RHS + RANK :]
    return jnp.concatenate([s1, s2, moved_on(s1), moved_on(s2)], axis=0)


def response_kernel(entering, rows, data, own, high_out, low_out, base_out):
    entering = [entering[j] for j in range(4)]
    state = own[:RHS]
    to_device = jnp.concatenate([state, device_gain(own[...])[: 2 * RANK]], axis=0)
    to_device = jnp.concatenate([moved_on(to_device), to_device], axis=0)
    for i in range(FAN):
        span = slice(BS * i, BS * (i + 1))
        s = own_piece(entering, i)
        both = jnp.concatenate([s, moved_on(s)], axis=0)
        y = times(both, split(rows[:, span]))
        gain = split(jnp.concatenate([y[RHS:ROWS], y[ROWS + RHS :]], axis=0))
        y = jnp.concatenate([y[ROWS : ROWS + RHS], y[:RHS]], axis=0)
        z = times(to_device, gain)
        base_out[:, span] = (
            data[:, span] + y + jnp.concatenate([z[:RHS], z[ROWS : ROWS + RHS]], axis=0)
        )
        gain = split(jnp.concatenate([z[ROWS + RHS :], z[RHS:ROWS]], axis=0))
        high_out[:, span] = gain[0]
        low_out[:, span] = gain[1]


def plane_kernel(place, *refs):
    *maps, half_out, own_out, received = refs
    chip, core = place[0], place[1]
    for n, ref in enumerate(maps):
        far, other = n % 4, n // 4
        at = 2 * ((chip - far) % 4) + jnp.where(other == 1, 1 - core, core)
        received[at] = ref[...]
    offsets, maps = unpack(received)
    entering, packed = sweeps(offsets, maps, True)
    half = jnp.where(core == 0, packed[: ROWS // 2], packed[ROWS // 2 :])
    for e in range(FAN):
        half_out[e] = half
    own_out[...] = own_piece(entering, 2 * chip + core)


def outputs_kernel(place, mine, other, high, low, base, first_out, second_out, received):
    core = place[1]
    at = pl.multiple_of(core * (ROWS // 2), 8)
    away = pl.multiple_of((1 - core) * (ROWS // 2), 8)
    for e in range(FAN):
        received[e, pl.ds(at, ROWS // 2)] = mine[e]
        received[e, pl.ds(away, ROWS // 2)] = other[e]
    offsets, maps = unpack(received)
    entering, _ = sweeps(offsets, maps, False)
    plane = own_piece(entering, place[2])
    both = jnp.concatenate([moved_on(plane), plane], axis=0)
    y = base[...] + times(both, (high[...], low[...]))
    first_out[...] = y[:RHS]
    second_out[...] = y[RHS:]


vmem = pl.BlockSpec(memory_space=pltpu.VMEM)
smem = pl.BlockSpec(memory_space=pltpu.SMEM)
hbm = pl.BlockSpec(memory_space=pltpu.HBM)


def call(kernel, name, out, specs, args, scratch=(), mib=16):
    return pl.pallas_call(
        kernel,
        out_shape=out,
        in_specs=specs,
        out_specs=jax.tree.map(lambda _: vmem, out),
        scratch_shapes=scratch,
        compiler_params=pltpu.CompilerParams(vmem_limit_bytes=mib << 20),
        name=name,
    )(*args)


def shape(*dims, dtype=f32):
    return jax.ShapeDtypeStruct(dims, dtype)


def local(
    right_sides, lower_inverse, lower_left, lower_right, upper_inverse, upper_left, upper_right, block_ranks
):
    order = right_sides.shape[1]
    index = lax.axis_index("rows")
    chip, core, plane = index % FAN // 2, index % 2, index // FAN
    place = jnp.stack([chip, core, plane]).astype(jnp.int32)
    n = lax.axis_size("rows")
    across = [[p * FAN + d for p in range(n // FAN)] for d in range(FAN)]
    to_core = [(i, i ^ 1) for i in range(n)]

    def along_y(far):
        return [(i, i // FAN * FAN + (i + 2 * far) % FAN) for i in range(n)]

    turned = [
        jnp.swapaxes(w, 1, 2) for w in (lower_left, lower_right, upper_left, upper_right)
    ]
    thin = pltpu.VMEM((FAN, RANK, BS), bf16)
    square = pltpu.VMEM((FAN, BS, BS), bf16)
    packed, entering, rows, data = call(
        pieces_kernel,
        "pieces",
        (
            shape(ROWS, 128),
            shape(4, ROWS, WIDE),
            shape(4 * RANK, order),
            shape(2 * RHS, order),
        ),
        [hbm] * 8,
        [
            pltpu.with_memory_space_constraint(x, pltpu.HBM)
            for x in (
                block_ranks, right_sides, lower_inverse, *turned[:2], upper_inverse, *turned[2:]
            )
        ],
        [
            pltpu.SMEM(block_ranks.shape, jnp.int32), pltpu.VMEM((RHS, order), bf16), square, thin, thin, square, thin, thin,
            pltpu.SemaphoreType.DMA((6 + 2 * FAN,)),
        ],
    )
    chips = [packed] + [lax.ppermute(packed, "rows", along_y(far)) for far in (1, 2, 3)]
    others = [lax.ppermute(x, "rows", to_core) for x in chips]
    half, own = call(
        plane_kernel,
        "plane",
        (shape(FAN, ROWS // 2, 128), shape(ROWS, 128)),
        [smem] + [vmem] * 8,
        (place, *chips, *others),
        [pltpu.VMEM((FAN, ROWS, 128), f32)],
    )
    mine = lax.all_to_all(half, "rows", 0, 0, tiled=True, axis_index_groups=across)
    high, low, base = call(
        response_kernel,
        "response",
        (shape(4 * RANK, order, dtype=bf16), shape(4 * RANK, order, dtype=bf16), shape(2 * RHS, order)),
        [vmem] * 4,
        (entering, rows, data, own),
    )
    mine, high, low, base = lax.optimization_barrier((mine, high, low, base))
    other = lax.ppermute(mine, "rows", to_core)
    return call(
        outputs_kernel,
        "outputs",
        (shape(RHS, order), shape(RHS, order)),
        [smem] + [vmem] * 5,
        (place, mine, other, high, low, base),
        [pltpu.VMEM((FAN, ROWS, 128), f32)],
    )


def solution(mesh):
    placed_in = (
        P("rhs", "rows"),
        P("rows", None, None),
        P("rows", None, None),
        P("rows", None, None),
        P("rows", None, None),
        P("rows", None, None),
        P("rows", None, None),
        P(None, "rows"),
    )
    return jax.shard_map(
        local,
        mesh=mesh,
        in_specs=placed_in,
        out_specs=(P("rhs", "rows"), P("rhs", "rows")),
        check_vma=False,
    )
```

```python
import functools

import jax
import jax.numpy as jnp
from jax import lax
from jax.experimental import pallas as pl
from jax.experimental.pallas import tpu as pltpu
from jax.sharding import PartitionSpec as P

f32, bf16 = jnp.float32, jnp.bfloat16

BS = 256
RANK = 32
RHS = 16
FAN = 8
WIDE = FAN * RANK
ROWS = RHS + 2 * RANK


def roll(x, shift):
    shift %= x.shape[1]
    return pltpu.roll(x, shift, 1) if shift else x


def split(x):
    high = x.astype(bf16)
    return high, (x - high.astype(f32)).astype(bf16)


def dot_nn(x, w):
    return lax.dot_general(x, w, (((1,), (0,)), ((), ())), preferred_element_type=f32)


def dot_nt(x, w):
    return lax.dot_general(x, w, (((1,), (1,)), ((), ())), preferred_element_type=f32)


def wide_times_exact(x, w, dot):
    n = x.shape[0]
    both = dot(jnp.concatenate(split(x), axis=0), w)
    return both[:n] + both[n:]


def times(x, w):
    n = x.shape[0]
    high, low = split(x)
    both = dot_nn(jnp.concatenate([high, low], axis=0), w[0])
    return both[:n] + both[n:] + dot_nn(high, w[1])


def block_ids(shape):
    return (
        lax.broadcasted_iota(jnp.int32, shape, 0) // RANK,
        lax.broadcasted_iota(jnp.int32, shape, 1) // RANK,
    )


def placed(tiled, offset):
    tiled = jnp.concatenate([tiled, tiled], axis=1)
    row, col = block_ids(tiled.shape)
    return jnp.where(col == row + offset, tiled, 0.0)


def below(x, rows):
    return jnp.concatenate([x, jnp.zeros((rows - x.shape[0], x.shape[1]), x.dtype)], axis=0)


def above(x, rows):
    return jnp.concatenate([jnp.zeros((rows - x.shape[0], x.shape[1]), x.dtype), x], axis=0)


def carries(t, r):
    one = (
        lax.broadcasted_iota(jnp.int32, (WIDE, WIDE), 0)
        == lax.broadcasted_iota(jnp.int32, (WIDE, WIDE), 1)
    ).astype(f32)
    sides = ((placed(t, 1), below, lambda x, n: x[: WIDE - n * RANK]),
             (placed(r, -1), above, lambda x, n: x[n * RANK :]))
    hops = [hop for hop, _, _ in sides]
    parts = [split(hop) for hop in hops]
    twos = [fill(times(cut(hop, 2), p), WIDE) for (hop, fill, cut), p in zip(sides, parts)]
    parts = [split(two) for two in twos]
    fours = [fill(times(cut(two, 4), p), WIDE) for two, (_, fill, cut), p in zip(twos, sides, parts)]
    threes = [fill(times(cut(hop, 3), p), WIDE) for (hop, fill, cut), p in zip(sides, parts)]
    out = []
    for hop, two, three, four, (_, fill, cut) in zip(hops, twos, threes, fours, sides):
        near = one + hop + two + three
        out.append(near + fill(times(cut(near, 4), split(four)), WIDE))
    return out


def sweeps(offsets, maps, outward, ends=None):
    o1, o2, o3, o4 = offsets
    t, r, a21, a31, a32, a41, a42 = maps
    up, down = carries(t, r) if ends is None else ends
    gap = jnp.zeros((RANK, WIDE), f32)
    up_next = split(jnp.concatenate([up[RANK:], gap], axis=0))
    down_next = split(jnp.concatenate([gap, down[:-RANK]], axis=0))
    d21, d31, d32, d41, d42 = (split(placed(a, 0)) for a in (a21, a31, a32, a41, a42))

    def with_rows(x, rows):
        if not outward:
            return x
        return jnp.concatenate([x, jnp.zeros((rows - x.shape[0], WIDE), f32)], axis=0)

    e1 = times(o1, up_next)
    if outward:
        e1 = jnp.concatenate([e1, up[:RANK]], axis=0)
    q2 = with_rows(o2, RHS + RANK) + times(e1, d21)
    e2 = times(q2, down_next)
    if outward:
        e2 = jnp.concatenate([e2, down[-RANK:]], axis=0)
    q3 = with_rows(o3, ROWS) + with_rows(times(e1, d31), ROWS) + times(e2, d32)
    e3 = times(q3, up_next)
    q4 = with_rows(o4, ROWS) + with_rows(times(e1, d41), ROWS) + times(e2, d42) + times(e3, d21)
    e4 = times(q4, down_next)
    entering = (e1, e2, e3, e4)
    if not outward:
        return entering, None
    dt, dr = split(placed(t, 0)), split(placed(r, 0))
    last, first = slice(128, 256), slice(0, 128)
    group = lax.broadcasted_iota(jnp.int32, (ROWS, 128), 1) // RANK
    t1 = roll(with_rows(with_rows(o1, RHS + RANK) + times(e1, dt), ROWS)[:, last], 32)
    t2 = roll((with_rows(q2, ROWS) + times(e2, dr))[:, first], 32)
    t3 = roll((q3 + times(e3, dt))[:, last], 96)
    t4 = roll((q4 + times(e4, dr))[:, first], 96)
    packed = jnp.where(
        group == 0, t1, jnp.where(group == 1, t2, jnp.where(group == 2, t3, t4))
    )
    return entering, packed


def unpack(received):
    own = received[:, RHS : RHS + RANK].reshape(WIDE, 128)
    cross = received[:, RHS + RANK :].reshape(WIDE, 128)
    lane_group = lax.broadcasted_iota(jnp.int32, (WIDE, 128), 1) // RANK

    def tiled(x, group):
        x = jnp.where(lane_group == group, x, 0.0)
        x = x + roll(x, 32)
        return x + roll(x, 64)

    maps = (
        tiled(own, 0),
        tiled(cross, 1),
        tiled(own, 1),
        tiled(own, 2),
        tiled(cross, 2),
        tiled(own, 3),
        tiled(cross, 3),
    )
    group = lax.broadcasted_iota(jnp.int32, (RHS, 128), 1) // RANK
    offsets = []
    for k in range(4):
        halves = []
        for half in range(2):
            out = jnp.zeros((RHS, 128), f32)
            for g in range(4):
                moved = roll(received[4 * half + g, :RHS], 32 * (g - k))
                out = jnp.where(group == g, moved, out)
            halves.append(out)
        offsets.append(jnp.concatenate(halves, axis=1))
    return tuple(offsets), maps


def own_piece(entering, piece):
    rows = entering[-1].shape[0]
    col = lax.broadcasted_iota(jnp.int32, (rows, WIDE), 1) // RANK
    group = lax.broadcasted_iota(jnp.int32, (rows, 128), 1) // RANK
    out = jnp.zeros((rows, 128), f32)
    for k, e in enumerate(entering):
        if e.shape[0] < rows:
            e = jnp.concatenate([e, jnp.zeros((rows - e.shape[0], WIDE), f32)], axis=0)
        e = jnp.where(col == piece, e, 0.0)
        e = e[:, :128] + e[:, 128:]
        e = e + roll(e, 32)
        e = e + roll(e, 64)
        out = jnp.where(group == k, e, out)
    return out


def moved_on(x):
    return jnp.where(lax.broadcasted_iota(jnp.int32, x.shape, 1) >= 64, roll(x, 64), 0.0)


def pieces_kernel(
    ranks_any, v_any, li_any, ll_any, lr_any, ui_any, ul_any, ur_any,
    packed_out, entering_out, rows_out, data_out,
    ranks, v, li, ll, lr, ui, ul, ur, sems,
):
    copies = {}

    def start(name, source, target, at):
        copies[name] = pltpu.make_async_copy(source, target, sems.at[at])
        copies[name].start()

    start("v", v_any, v, 0)
    start("ll", ll_any, ll, 1)
    for i in range(FAN):
        start(("a", i), li_any.at[i], li.at[i], 6 + i)
    start("ul", ul_any, ul, 2)
    for i in range(FAN):
        start(("b", i), ui_any.at[i], ui.at[i], 6 + FAN + i)
    start("lr", lr_any, lr, 3)
    start("ur", ur_any, ur, 4)
    start("ranks", ranks_any, ranks, 5)

    group = lax.broadcasted_iota(jnp.int32, (RHS, 128), 1) // RANK
    eye = (
        lax.broadcasted_iota(jnp.int32, (RANK, 128), 0)
        == lax.broadcasted_iota(jnp.int32, (RANK, 128), 1) % RANK
    ).astype(f32)
    blocks = range(FAN)
    span = [slice(BS * i, BS * (i + 1)) for i in blocks]
    k = RHS + RANK
    va, c, d, vab, cb, last, four = ([None] * FAN for _ in range(7))
    def masked(right, rank):
        keep = lax.broadcasted_iota(jnp.int32, (RANK, BS), 0) < rank
        w = jnp.where(keep, right.astype(f32), 0.0).astype(bf16)
        return jnp.concatenate([w] * 4, axis=0)

    copies["v"].wait()
    copies["ll"].wait()
    for i in blocks:
        copies["a", i].wait()
        one = dot_nt(jnp.concatenate([v[:, span[i]], ll[i]], axis=0), li[i])
        va[i] = one[:RHS]
        c[i] = (-one[RHS:]).astype(bf16)
    copies["ul"].wait()
    for i in blocks:
        copies["b", i].wait()
        two = dot_nt(jnp.concatenate([*split(va[i]), c[i], ul[i]], axis=0), ui[i])
        vab[i] = two[:RHS] + two[RHS : 2 * RHS]
        cb[i] = two[2 * RHS : 2 * RHS + RANK]
        d[i] = (-two[2 * RHS + RANK :]).astype(bf16)
    copies["lr"].wait()
    copies["ur"].wait()
    copies["ranks"].wait()
    m = [masked(lr[i], ranks[0, i]) for i in blocks]
    n = [masked(ur[i], ranks[1, i]) for i in blocks]
    t = jnp.concatenate([eye + dot_nt(c[i], m[i]) for i in blocks], axis=0)
    r = jnp.concatenate([eye + dot_nt(d[i], n[i]) for i in blocks], axis=0)
    for i in blocks:
        both = split(jnp.concatenate([vab[i], cb[i]], axis=0))
        three = dot_nt(jnp.concatenate([*both, d[i]], axis=0), li[i])
        last[i] = jnp.concatenate([three[:k] + three[k : 2 * k], three[2 * k :]], axis=0)
    ends = carries(t, r)
    for i in blocks:
        four[i] = wide_times_exact(last[i], ui[i], dot_nt)
        rows_out[:, span[i]] = jnp.concatenate([four[i][RHS:], cb[i], d[i].astype(f32)], axis=0)
        data_out[:, span[i]] = jnp.concatenate([vab[i], four[i][:RHS]], axis=0)
    offsets = [[jnp.zeros((RHS, 128), f32)] * 2 for _ in range(4)]
    maps = [[] for _ in range(5)]
    for i in blocks:
        lo = wide_times_exact(jnp.concatenate([va[i], last[i]], axis=0), m[i], dot_nt)
        hi = wide_times_exact(jnp.concatenate([vab[i], cb[i], four[i]], axis=0), n[i], dot_nt)
        o = (lo[:RHS], hi[:RHS], lo[RHS : 2 * RHS], hi[k : k + RHS])
        for j in range(4):
            offsets[j][i // 4] = jnp.where(group == i % 4, o[j], offsets[j][i // 4])
        maps[0].append(hi[RHS:k])
        maps[1].append(lo[2 * RHS : 2 * RHS + RANK])
        maps[2].append(lo[2 * RHS + RANK :])
        maps[3].append(hi[k + RHS : k + RHS + RANK])
        maps[4].append(hi[k + RHS + RANK :])
    offsets = [jnp.concatenate(o, axis=1) for o in offsets]
    maps = [t, r] + [jnp.concatenate(m, axis=0) for m in maps]
    entering, packed = sweeps(offsets, maps, True, ends)
    packed_out[...] = packed
    for j, e in enumerate(entering):
        entering_out[j, : e.shape[0]] = e
        if e.shape[0] < ROWS:
            entering_out[j, e.shape[0] :] = jnp.zeros((ROWS - e.shape[0], WIDE), f32)


def response_kernel(entering, rows, data, high_out, low_out, base_out):
    entering = [entering[j] for j in range(4)]
    for i in range(FAN):
        span = slice(BS * i, BS * (i + 1))
        s = own_piece(entering, i)
        both = jnp.concatenate([s, moved_on(s)], axis=0)
        y = times(both, split(rows[:, span]))
        base_out[:, span] = data[:, span] + jnp.concatenate(
            [y[ROWS : ROWS + RHS], y[:RHS]], axis=0
        )
        gain = split(jnp.concatenate([y[RHS:ROWS], y[ROWS + RHS :]], axis=0))
        high_out[:, span] = gain[0]
        low_out[:, span] = gain[1]


def device_gain(own):
    s1, s2 = own[RHS : RHS + RANK], own[RHS + RANK :]
    return jnp.concatenate([s1, s2, moved_on(s1), moved_on(s2)], axis=0)


def plane_kernel(place, *refs):
    *maps, half_out, own_out, received = refs
    chip, core = place[0], place[1]
    for n, ref in enumerate(maps):
        far, other = n % 4, n // 4
        at = 2 * ((chip - far) % 4) + jnp.where(other == 1, 1 - core, core)
        received[at] = ref[...]
    offsets, maps = unpack(received)
    entering, packed = sweeps(offsets, maps, True)
    half = jnp.where(core == 0, packed[: ROWS // 2], packed[ROWS // 2 :])
    for e in range(FAN):
        half_out[e] = half
    own_out[...] = own_piece(entering, 2 * chip + core)


def outputs_kernel(place, mine, other, own, high, low, base, first_out, second_out, received):
    core = place[1]
    at = pl.multiple_of(core * (ROWS // 2), 8)
    away = pl.multiple_of((1 - core) * (ROWS // 2), 8)
    for e in range(FAN):
        received[e, pl.ds(at, ROWS // 2)] = mine[e]
        received[e, pl.ds(away, ROWS // 2)] = other[e]
    offsets, maps = unpack(received)
    entering, _ = sweeps(offsets, maps, False)
    plane = own_piece(entering, place[2])
    own = own[...]
    state = own[:RHS] + times(plane, split(device_gain(own)))
    both = jnp.concatenate([moved_on(state), state], axis=0)
    y = base[...] + times(both, (high[...], low[...]))
    first_out[...] = y[:RHS]
    second_out[...] = y[RHS:]


vmem = pl.BlockSpec(memory_space=pltpu.VMEM)
smem = pl.BlockSpec(memory_space=pltpu.SMEM)
hbm = pl.BlockSpec(memory_space=pltpu.HBM)


def call(kernel, name, out, specs, args, scratch=(), mib=16):
    return pl.pallas_call(
        kernel,
        out_shape=out,
        in_specs=specs,
        out_specs=jax.tree.map(lambda _: vmem, out),
        scratch_shapes=scratch,
        compiler_params=pltpu.CompilerParams(vmem_limit_bytes=mib << 20),
        name=name,
    )(*args)


def shape(*dims, dtype=f32):
    return jax.ShapeDtypeStruct(dims, dtype)


def local(
    right_sides, lower_inverse, lower_left, lower_right, upper_inverse, upper_left, upper_right, block_ranks
):
    order = right_sides.shape[1]
    index = lax.axis_index("rows")
    chip, core, plane = index % FAN // 2, index % 2, index // FAN
    place = jnp.stack([chip, core, plane]).astype(jnp.int32)
    n = lax.axis_size("rows")
    across = [[p * FAN + d for p in range(n // FAN)] for d in range(FAN)]
    to_core = [(i, i ^ 1) for i in range(n)]

    def along_y(far):
        return [(i, i // FAN * FAN + (i + 2 * far) % FAN) for i in range(n)]

    turned = [
        jnp.swapaxes(w, 1, 2) for w in (lower_left, lower_right, upper_left, upper_right)
    ]
    thin = pltpu.VMEM((FAN, RANK, BS), bf16)
    square = pltpu.VMEM((FAN, BS, BS), bf16)
    packed, entering, rows, data = call(
        pieces_kernel,
        "pieces",
        (
            shape(ROWS, 128),
            shape(4, ROWS, WIDE),
            shape(4 * RANK, order),
            shape(2 * RHS, order),
        ),
        [hbm] * 8,
        [
            pltpu.with_memory_space_constraint(x, pltpu.HBM)
            for x in (
                block_ranks, right_sides, lower_inverse, *turned[:2], upper_inverse, *turned[2:]
            )
        ],
        [
            pltpu.SMEM(block_ranks.shape, jnp.int32), pltpu.VMEM((RHS, order), bf16), square, thin, thin, square, thin, thin,
            pltpu.SemaphoreType.DMA((6 + 2 * FAN,)),
        ],
    )
    chips = [packed] + [lax.ppermute(packed, "rows", along_y(far)) for far in (1, 2, 3)]
    high, low, base = call(
        response_kernel,
        "response",
        (shape(4 * RANK, order, dtype=bf16), shape(4 * RANK, order, dtype=bf16), shape(2 * RHS, order)),
        [vmem] * 3,
        (entering, rows, data),
    )
    *chips, high, low, base = lax.optimization_barrier((*chips, high, low, base))
    others = [lax.ppermute(x, "rows", to_core) for x in chips]
    half, own = call(
        plane_kernel,
        "plane",
        (shape(FAN, ROWS // 2, 128), shape(ROWS, 128)),
        [smem] + [vmem] * 8,
        (place, *chips, *others),
        [pltpu.VMEM((FAN, ROWS, 128), f32)],
    )
    mine = lax.all_to_all(half, "rows", 0, 0, tiled=True, axis_index_groups=across)
    other = lax.ppermute(mine, "rows", to_core)
    return call(
        outputs_kernel,
        "outputs",
        (shape(RHS, order), shape(RHS, order)),
        [smem] + [vmem] * 6,
        (place, mine, other, own, high, low, base),
        [pltpu.VMEM((FAN, ROWS, 128), f32)],
    )


def solution(mesh):
    placed_in = (
        P("rhs", "rows"),
        P("rows", None, None),
        P("rows", None, None),
        P("rows", None, None),
        P("rows", None, None),
        P("rows", None, None),
        P("rows", None, None),
        P(None, "rows"),
    )
    return jax.shard_map(
        local,
        mesh=mesh,
        in_specs=placed_in,
        out_specs=(P("rhs", "rows"), P("rhs", "rows")),
        check_vma=False,
    )
```

```python
import functools

import jax
import jax.numpy as jnp
from jax import lax
from jax.experimental import pallas as pl
from jax.experimental.pallas import tpu as pltpu
from jax.sharding import PartitionSpec as P

f32, bf16 = jnp.float32, jnp.bfloat16

BS = 256
RANK = 32
RHS = 16
FAN = 8
WIDE = FAN * RANK
ROWS = RHS + 2 * RANK


def roll(x, shift):
    shift %= x.shape[1]
    return pltpu.roll(x, shift, 1) if shift else x


def split(x):
    high = x.astype(bf16)
    return high, (x - high.astype(f32)).astype(bf16)


def dot_nn(x, w):
    return lax.dot_general(x, w, (((1,), (0,)), ((), ())), preferred_element_type=f32)


def dot_nt(x, w):
    return lax.dot_general(x, w, (((1,), (1,)), ((), ())), preferred_element_type=f32)


def wide_times_exact(x, w, dot):
    n = x.shape[0]
    both = dot(jnp.concatenate(split(x), axis=0), w)
    return both[:n] + both[n:]


def stacked(x):
    high, low = split(x)
    return jnp.concatenate([high, low], axis=0), high


def times_parts(x, w):
    n = x[1].shape[0]
    both = dot_nn(x[0], w[0])
    return both[:n] + both[n:] + dot_nn(x[1], w[1])


def times(x, w):
    return times_parts(stacked(x), w)


def block_ids(shape):
    return (
        lax.broadcasted_iota(jnp.int32, shape, 0) // RANK,
        lax.broadcasted_iota(jnp.int32, shape, 1) // RANK,
    )


def placed(tiled, offset):
    tiled = jnp.concatenate([tiled, tiled], axis=1)
    row, col = block_ids(tiled.shape)
    return jnp.where(col == row + offset, tiled, 0.0)


def below(x, rows):
    return jnp.concatenate([x, jnp.zeros((rows - x.shape[0], x.shape[1]), x.dtype)], axis=0)


def above(x, rows):
    return jnp.concatenate([jnp.zeros((rows - x.shape[0], x.shape[1]), x.dtype), x], axis=0)


def carries(t, r):
    one = (
        lax.broadcasted_iota(jnp.int32, (WIDE, WIDE), 0)
        == lax.broadcasted_iota(jnp.int32, (WIDE, WIDE), 1)
    ).astype(f32)
    sides = ((placed(t, 1), below, lambda x, n: x[: WIDE - n * RANK]),
             (placed(r, -1), above, lambda x, n: x[n * RANK :]))
    hops = [hop for hop, _, _ in sides]
    parts = [split(hop) for hop in hops]
    twos = [fill(times(cut(hop, 2), p), WIDE) for (hop, fill, cut), p in zip(sides, parts)]
    parts = [split(two) for two in twos]
    fours = [fill(times(cut(two, 4), p), WIDE) for two, (_, fill, cut), p in zip(twos, sides, parts)]
    threes = [fill(times(cut(hop, 3), p), WIDE) for (hop, fill, cut), p in zip(sides, parts)]
    out = []
    for hop, two, three, four, (_, fill, cut) in zip(hops, twos, threes, fours, sides):
        near = one + hop + two + three
        out.append(near + fill(times(cut(near, 4), split(four)), WIDE))
    return out


def sweeps(offsets, maps, outward, ends=None):
    o1, o2, o3, o4 = offsets
    t, r, a21, a31, a32, a41, a42 = maps
    up, down = carries(t, r) if ends is None else ends
    gap = jnp.zeros((RANK, WIDE), f32)
    up_next = split(jnp.concatenate([up[RANK:], gap], axis=0))
    down_next = split(jnp.concatenate([gap, down[:-RANK]], axis=0))
    d21, d31, d32, d41, d42 = (split(placed(a, 0)) for a in (a21, a31, a32, a41, a42))

    def with_rows(x, rows):
        if not outward:
            return x
        return jnp.concatenate([x, jnp.zeros((rows - x.shape[0], WIDE), f32)], axis=0)

    e1 = times(o1, up_next)
    if outward:
        e1 = jnp.concatenate([e1, up[:RANK]], axis=0)
    e1_parts = stacked(e1)
    q2 = with_rows(o2, RHS + RANK) + times_parts(e1_parts, d21)
    e2 = times(q2, down_next)
    g31, g41 = times_parts(e1_parts, d31), times_parts(e1_parts, d41)
    if outward:
        dt, dr = split(placed(t, 0)), split(placed(r, 0))
        g1 = times_parts(e1_parts, dt)
        e2 = jnp.concatenate([e2, down[-RANK:]], axis=0)
    e2_parts = stacked(e2)
    q3 = with_rows(o3, ROWS) + with_rows(g31, ROWS) + times_parts(e2_parts, d32)
    e3 = times(q3, up_next)
    g42 = times_parts(e2_parts, d42)
    if outward:
        g2 = times_parts(e2_parts, dr)
    e3_parts = stacked(e3)
    q4 = with_rows(o4, ROWS) + with_rows(g41, ROWS) + g42 + times_parts(e3_parts, d21)
    e4 = times(q4, down_next)
    entering = (e1, e2, e3, e4)
    if not outward:
        return entering, None
    g3 = times_parts(e3_parts, dt)
    g4 = times(e4, dr)
    last, first = slice(128, 256), slice(0, 128)
    group = lax.broadcasted_iota(jnp.int32, (ROWS, 128), 1) // RANK
    t1 = roll(with_rows(with_rows(o1, RHS + RANK) + g1, ROWS)[:, last], 32)
    t2 = roll((with_rows(q2, ROWS) + g2)[:, first], 32)
    t3 = roll((q3 + g3)[:, last], 96)
    t4 = roll((q4 + g4)[:, first], 96)
    packed = jnp.where(
        group == 0, t1, jnp.where(group == 1, t2, jnp.where(group == 2, t3, t4))
    )
    return entering, packed


def unpack(received, fine=None):
    own = received[:, RHS : RHS + RANK].reshape(WIDE, 128)
    cross = received[:, RHS + RANK :].reshape(WIDE, 128)
    lane_group = lax.broadcasted_iota(jnp.int32, (WIDE, 128), 1) // RANK

    def tiled(x, group):
        x = jnp.where(lane_group[: x.shape[0]] == group, x, 0.0)
        x = x + roll(x, 32)
        return x + roll(x, 64)

    t, r = tiled(own, 0), tiled(cross, 1)
    if fine is not None:
        half = RANK // 2
        low = [tiled(fine.reshape(FAN * half, 128), g).reshape(FAN, half, 128) for g in range(4)]
        t = t + jnp.concatenate(low[:2], axis=1).reshape(WIDE, 128)
        r = r + jnp.concatenate(low[2:], axis=1).reshape(WIDE, 128)
    maps = (
        t,
        r,
        tiled(own, 1),
        tiled(own, 2),
        tiled(cross, 2),
        tiled(own, 3),
        tiled(cross, 3),
    )
    group = lax.broadcasted_iota(jnp.int32, (RHS, 128), 1) // RANK
    offsets = []
    for k in range(4):
        halves = []
        for half in range(2):
            out = jnp.zeros((RHS, 128), f32)
            for g in range(4):
                moved = roll(received[4 * half + g, :RHS], 32 * (g - k))
                out = jnp.where(group == g, moved, out)
            halves.append(out)
        offsets.append(jnp.concatenate(halves, axis=1))
    return tuple(offsets), maps


def own_piece(entering, piece):
    rows = entering[-1].shape[0]
    col = lax.broadcasted_iota(jnp.int32, (rows, WIDE), 1) // RANK
    group = lax.broadcasted_iota(jnp.int32, (rows, 128), 1) // RANK
    out = jnp.zeros((rows, 128), f32)
    for k, e in enumerate(entering):
        if e.shape[0] < rows:
            e = jnp.concatenate([e, jnp.zeros((rows - e.shape[0], WIDE), f32)], axis=0)
        e = jnp.where(col == piece, e, 0.0)
        e = e[:, :128] + e[:, 128:]
        e = e + roll(e, 32)
        e = e + roll(e, 64)
        out = jnp.where(group == k, e, out)
    return out


def moved_on(x):
    return jnp.where(lax.broadcasted_iota(jnp.int32, x.shape, 1) >= 64, roll(x, 64), 0.0)


def pieces_kernel(
    ranks_any, v_any, li_any, ll_any, lr_any, ui_any, ul_any, ur_any,
    packed_out, entering_out, rows_out, data_out,
    ranks, v, li, ll, lr, ui, ul, ur, sems,
):
    copies = {}

    def start(name, source, target, at):
        copies[name] = pltpu.make_async_copy(source, target, sems.at[at])
        copies[name].start()

    start("v", v_any, v, 0)
    start("ll", ll_any, ll, 1)
    start("a", li_any, li, 6)
    start("ul", ul_any, ul, 2)
    start("b", ui_any, ui, 7)
    start("lr", lr_any, lr, 3)
    start("ur", ur_any, ur, 4)
    start("ranks", ranks_any, ranks, 5)

    group = lax.broadcasted_iota(jnp.int32, (RHS, 128), 1) // RANK
    eye = (
        lax.broadcasted_iota(jnp.int32, (RANK, 128), 0)
        == lax.broadcasted_iota(jnp.int32, (RANK, 128), 1) % RANK
    ).astype(f32)
    blocks = range(FAN)
    span = [slice(BS * i, BS * (i + 1)) for i in blocks]
    k = RHS + RANK
    for name in ("v", "ll", "a"):
        copies[name].wait()
    va, c, d, vab, cb, last, four = ([None] * FAN for _ in range(7))
    def masked(right, rank):
        keep = lax.broadcasted_iota(jnp.int32, (RANK, BS), 0) < rank
        w = jnp.where(keep, right.astype(f32), 0.0).astype(bf16)
        return jnp.concatenate([w] * 4, axis=0)

    for i in blocks:
        one = dot_nt(jnp.concatenate([v[:, span[i]], ll[i]], axis=0), li[i])
        va[i] = one[:RHS]
        c[i] = (-one[RHS:]).astype(bf16)
    for name in ("ul", "b", "lr", "ur", "ranks"):
        copies[name].wait()
    for i in blocks:
        two = dot_nt(jnp.concatenate([*split(va[i]), c[i], ul[i]], axis=0), ui[i])
        vab[i] = two[:RHS] + two[RHS : 2 * RHS]
        cb[i] = two[2 * RHS : 2 * RHS + RANK]
        d[i] = (-two[2 * RHS + RANK :]).astype(bf16)
    m = [masked(lr[i], ranks[0, i]) for i in blocks]
    n = [masked(ur[i], ranks[1, i]) for i in blocks]
    t = jnp.concatenate([eye + dot_nt(c[i], m[i]) for i in blocks], axis=0)
    r = jnp.concatenate([eye + dot_nt(d[i], n[i]) for i in blocks], axis=0)
    for i in blocks:
        both = split(jnp.concatenate([vab[i], cb[i]], axis=0))
        three = dot_nt(jnp.concatenate([*both, d[i]], axis=0), li[i])
        last[i] = jnp.concatenate([three[:k] + three[k : 2 * k], three[2 * k :]], axis=0)
    ends = carries(t, r)
    for i in blocks:
        four[i] = wide_times_exact(last[i], ui[i], dot_nt)
        rows_out[:, span[i]] = jnp.concatenate([four[i][RHS:], cb[i], d[i].astype(f32)], axis=0)
        data_out[:, span[i]] = jnp.concatenate([vab[i], four[i][:RHS]], axis=0)
    offsets = [[jnp.zeros((RHS, 128), f32)] * 2 for _ in range(4)]
    maps = [[] for _ in range(5)]
    for i in blocks:
        lo = wide_times_exact(jnp.concatenate([va[i], last[i]], axis=0), m[i], dot_nt)
        hi = wide_times_exact(jnp.concatenate([vab[i], cb[i], four[i]], axis=0), n[i], dot_nt)
        o = (lo[:RHS], hi[:RHS], lo[RHS : 2 * RHS], hi[k : k + RHS])
        for j in range(4):
            offsets[j][i // 4] = jnp.where(group == i % 4, o[j], offsets[j][i // 4])
        maps[0].append(hi[RHS:k])
        maps[1].append(lo[2 * RHS : 2 * RHS + RANK])
        maps[2].append(lo[2 * RHS + RANK :])
        maps[3].append(hi[k + RHS : k + RHS + RANK])
        maps[4].append(hi[k + RHS + RANK :])
    offsets = [jnp.concatenate(o, axis=1) for o in offsets]
    maps = [t, r] + [jnp.concatenate(m, axis=0) for m in maps]
    entering, packed = sweeps(offsets, maps, True, ends)
    packed_out[...] = packed
    for j, e in enumerate(entering):
        entering_out[j, : e.shape[0]] = e
        if e.shape[0] < ROWS:
            entering_out[j, e.shape[0] :] = jnp.zeros((ROWS - e.shape[0], WIDE), f32)


def response_kernel(entering, rows, data, high_out, low_out, base_out):
    entering = [entering[j] for j in range(4)]
    for i in range(FAN):
        span = slice(BS * i, BS * (i + 1))
        s = own_piece(entering, i)
        both = jnp.concatenate([s, moved_on(s)], axis=0)
        y = times(both, split(rows[:, span]))
        base_out[:, span] = data[:, span] + jnp.concatenate(
            [y[ROWS : ROWS + RHS], y[:RHS]], axis=0
        )
        gain = split(jnp.concatenate([y[RHS:ROWS], y[ROWS + RHS :]], axis=0))
        high_out[:, span] = gain[0]
        low_out[:, span] = gain[1]


def device_gain(own):
    s1, s2 = own[RHS : RHS + RANK], own[RHS + RANK :]
    return jnp.concatenate([s1, s2, moved_on(s1), moved_on(s2)], axis=0)


def plane_kernel(place, *refs):
    *maps, wire_out, own_out, received = refs
    chip, core = place[0], place[1]
    for n, ref in enumerate(maps):
        far, other = n % 4, n // 4
        at = 2 * ((chip - far) % 4) + jnp.where(other == 1, 1 - core, core)
        received[at] = ref[...]
    offsets, maps = unpack(received)
    entering, packed = sweeps(offsets, maps, True)
    high, low = split(packed)
    low = low.astype(f32)
    half, group = RANK // 2, lax.broadcasted_iota(jnp.int32, (RANK // 2, 128), 1) // RANK
    t1, t2 = low[RHS : RHS + half], roll(low[RHS + half : RHS + RANK], 32)
    r1, r2 = roll(low[RHS + RANK : ROWS - half], 32), roll(low[ROWS - half :], 64)
    fine = jnp.where(group == 0, t1, jnp.where(group == 1, t2, jnp.where(group == 2, r1, r2)))
    fine = fine.astype(bf16)
    for e in range(FAN):
        wire_out[e, :ROWS] = high
        wire_out[e, ROWS:] = fine
    own_out[...] = own_piece(entering, 2 * chip + core)


def outputs_kernel(place, received, own, high, low, base, first_out, second_out):
    offsets, maps = unpack(received[:, :ROWS].astype(f32), received[:, ROWS:].astype(f32))
    entering, _ = sweeps(offsets, maps, False)
    plane = own_piece(entering, place[2])
    own = own[...]
    state = own[:RHS] + times(plane, split(device_gain(own)))
    both = jnp.concatenate([moved_on(state), state], axis=0)
    y = base[...] + times(both, (high[...], low[...]))
    first_out[...] = y[:RHS]
    second_out[...] = y[RHS:]


vmem = pl.BlockSpec(memory_space=pltpu.VMEM)
smem = pl.BlockSpec(memory_space=pltpu.SMEM)
hbm = pl.BlockSpec(memory_space=pltpu.HBM)


def call(kernel, name, out, specs, args, scratch=(), mib=16):
    return pl.pallas_call(
        kernel,
        out_shape=out,
        in_specs=specs,
        out_specs=jax.tree.map(lambda _: vmem, out),
        scratch_shapes=scratch,
        compiler_params=pltpu.CompilerParams(vmem_limit_bytes=mib << 20),
        name=name,
    )(*args)


def shape(*dims, dtype=f32):
    return jax.ShapeDtypeStruct(dims, dtype)


def local(
    right_sides, lower_inverse, lower_left, lower_right, upper_inverse, upper_left, upper_right, block_ranks
):
    order = right_sides.shape[1]
    index = lax.axis_index("rows")
    chip, core, plane = index % FAN // 2, index % 2, index // FAN
    place = jnp.stack([chip, core, plane]).astype(jnp.int32)
    n = lax.axis_size("rows")
    across = [[p * FAN + d for p in range(n // FAN)] for d in range(FAN)]
    to_core = [(i, i ^ 1) for i in range(n)]

    def along_y(far):
        return [(i, i // FAN * FAN + (i + 2 * far) % FAN) for i in range(n)]

    turned = [
        jnp.swapaxes(w, 1, 2) for w in (lower_left, lower_right, upper_left, upper_right)
    ]
    thin = pltpu.VMEM((FAN, RANK, BS), bf16)
    square = pltpu.VMEM((FAN, BS, BS), bf16)
    packed, entering, rows, data = call(
        pieces_kernel,
        "pieces",
        (
            shape(ROWS, 128),
            shape(4, ROWS, WIDE),
            shape(4 * RANK, order),
            shape(2 * RHS, order),
        ),
        [hbm] * 8,
        [
            pltpu.with_memory_space_constraint(x, pltpu.HBM)
            for x in (
                block_ranks, right_sides, lower_inverse, *turned[:2], upper_inverse, *turned[2:]
            )
        ],
        [
            pltpu.SMEM(block_ranks.shape, jnp.int32), pltpu.VMEM((RHS, order), bf16), square, thin, thin, square, thin, thin,
            pltpu.SemaphoreType.DMA((8,)),
        ],
    )
    chips = [packed] + [lax.ppermute(packed, "rows", along_y(far)) for far in (1, 2, 3)]
    high, low, base = call(
        response_kernel,
        "response",
        (shape(4 * RANK, order, dtype=bf16), shape(4 * RANK, order, dtype=bf16), shape(2 * RHS, order)),
        [vmem] * 3,
        (entering, rows, data),
    )
    chips[2], high, low, base = lax.optimization_barrier((chips[2], high, low, base))
    others = [lax.ppermute(x, "rows", to_core) for x in chips]
    wire, own = call(
        plane_kernel,
        "plane",
        (shape(FAN, ROWS + RANK // 2, 128, dtype=bf16), shape(ROWS, 128)),
        [smem] + [vmem] * 8,
        (place, *chips, *others),
        [pltpu.VMEM((FAN, ROWS, 128), f32)],
    )
    received = lax.all_to_all(wire, "rows", 0, 0, tiled=True, axis_index_groups=across)
    return call(
        outputs_kernel,
        "outputs",
        (shape(RHS, order), shape(RHS, order)),
        [smem] + [vmem] * 5,
        (place, received, own, high, low, base),
    )


def solution(mesh):
    placed_in = (
        P("rhs", "rows"),
        P("rows", None, None),
        P("rows", None, None),
        P("rows", None, None),
        P("rows", None, None),
        P("rows", None, None),
        P("rows", None, None),
        P(None, "rows"),
    )
    return jax.shard_map(
        local,
        mesh=mesh,
        in_specs=placed_in,
        out_specs=(P("rhs", "rows"), P("rhs", "rows")),
        check_vma=False,
    )
```

```python
import functools

import jax
import jax.numpy as jnp
from jax import lax
from jax.experimental import pallas as pl
from jax.experimental.pallas import tpu as pltpu
from jax.sharding import PartitionSpec as P

f32, bf16 = jnp.float32, jnp.bfloat16

BS = 256
RANK = 32
RHS = 16
FAN = 8
WIDE = FAN * RANK
ROWS = RHS + 2 * RANK
WIRE = ROWS + RANK // 2


def roll(x, shift):
    shift %= x.shape[1]
    return pltpu.roll(x, shift, 1) if shift else x


def split(x):
    high = x.astype(bf16)
    return high, (x - high.astype(f32)).astype(bf16)


def dot_nn(x, w):
    return lax.dot_general(x, w, (((1,), (0,)), ((), ())), preferred_element_type=f32)


def dot_nt(x, w):
    return lax.dot_general(x, w, (((1,), (1,)), ((), ())), preferred_element_type=f32)


def wide_times_exact(x, w, dot):
    n = x.shape[0]
    both = dot(jnp.concatenate(split(x), axis=0), w)
    return both[:n] + both[n:]


def stacked(x):
    high, low = split(x)
    return jnp.concatenate([high, low], axis=0), high


def times_parts(x, w):
    n = x[1].shape[0]
    both = dot_nn(x[0], w[0])
    out = both[:n] + both[n:]
    return out if w[1] is None else out + dot_nn(x[1], w[1])


def times(x, w):
    return times_parts(stacked(x), w)


def block_ids(shape):
    return (
        lax.broadcasted_iota(jnp.int32, shape, 0) // RANK,
        lax.broadcasted_iota(jnp.int32, shape, 1) // RANK,
    )


def placed(tiled, offset):
    tiled = jnp.concatenate([tiled, tiled], axis=1)
    row, col = block_ids(tiled.shape)
    return jnp.where(col == row + offset, tiled, 0.0)


def below(x, rows):
    return jnp.concatenate([x, jnp.zeros((rows - x.shape[0], x.shape[1]), x.dtype)], axis=0)


def above(x, rows):
    return jnp.concatenate([jnp.zeros((rows - x.shape[0], x.shape[1]), x.dtype), x], axis=0)


def joining(get, outward, exact):
    as_parts = (lambda w: (w.astype(bf16), None)) if exact else split
    one = (
        lax.broadcasted_iota(jnp.int32, (WIDE, WIDE), 0)
        == lax.broadcasted_iota(jnp.int32, (WIDE, WIDE), 1)
    ).astype(f32)
    sides = ((below, lambda x, n: x[: WIDE - n * RANK]), (above, lambda x, n: x[n * RANK :]))
    t, r = get("T"), get("R")
    hops = [placed(t, 1), placed(r, -1)]
    parts = [split(hop) for hop in hops]
    twos = [fill(times(cut(hop, 2), p), WIDE) for hop, p, (fill, cut) in zip(hops, parts, sides)]
    yield
    parts = [split(two) for two in twos]
    fours = [fill(times(cut(two, 4), p), WIDE) for two, p, (fill, cut) in zip(twos, parts, sides)]
    threes = [fill(times(cut(hop, 3), p), WIDE) for hop, p, (fill, cut) in zip(hops, parts, sides)]
    yield
    up, down = (
        near + fill(times(cut(near, 4), split(four)), WIDE)
        for near, four, (fill, cut) in zip(
            [one + hop + two + three for hop, two, three in zip(hops, twos, threes)], fours, sides
        )
    )
    yield
    gap = jnp.zeros((RANK, WIDE), f32)
    up_next = split(jnp.concatenate([up[RANK:], gap], axis=0))
    down_next = split(jnp.concatenate([gap, down[:-RANK]], axis=0))

    def with_rows(x, rows):
        return below(x, rows) if outward and x.shape[0] < rows else x

    e1 = times(get("o1"), up_next)
    d21 = as_parts(placed(get("A21"), 0))
    yield
    if outward:
        e1 = jnp.concatenate([e1, up[:RANK]], axis=0)
        dt, dr = split(placed(t, 0)), split(placed(r, 0))
    e1_parts = stacked(e1)
    q2 = with_rows(get("o2"), RHS + RANK) + times_parts(e1_parts, d21)
    yield
    e2 = times(q2, down_next)
    yield
    g31 = times_parts(e1_parts, as_parts(placed(get("A31"), 0)))
    if outward:
        g1 = times_parts(e1_parts, dt)
        e2 = jnp.concatenate([e2, down[-RANK:]], axis=0)
    e2_parts = stacked(e2)
    g32 = times_parts(e2_parts, as_parts(placed(get("A32"), 0)))
    yield
    q3 = with_rows(get("o3"), ROWS) + with_rows(g31, ROWS) + g32
    e3 = times(q3, up_next)
    yield
    g41 = times_parts(e1_parts, as_parts(placed(get("A41"), 0)))
    g42 = times_parts(e2_parts, as_parts(placed(get("A42"), 0)))
    if outward:
        g2 = times_parts(e2_parts, dr)
    e3_parts = stacked(e3)
    q4 = with_rows(get("o4"), ROWS) + with_rows(g41, ROWS) + g42 + times_parts(e3_parts, d21)
    yield
    e4 = times(q4, down_next)
    entering = (e1, e2, e3, e4)
    if not outward:
        return entering, None
    g3 = times_parts(e3_parts, dt)
    g4 = times(e4, dr)
    last, first = slice(128, 256), slice(0, 128)
    group = lax.broadcasted_iota(jnp.int32, (ROWS, 128), 1) // RANK
    t1 = roll(with_rows(with_rows(get("o1"), RHS + RANK) + g1, ROWS)[:, last], 32)
    t2 = roll((with_rows(q2, ROWS) + g2)[:, first], 32)
    t3 = roll((q3 + g3)[:, last], 96)
    t4 = roll((q4 + g4)[:, first], 96)
    packed = jnp.where(
        group == 0, t1, jnp.where(group == 1, t2, jnp.where(group == 2, t3, t4))
    )
    return entering, packed


def joined(parts, outward, exact, between=iter(()), every=0):
    steps = joining(parts, outward, exact)
    while True:
        try:
            next(steps)
        except StopIteration as end:
            return end.value
        for _ in range(every):
            next(between, None)


def to_wire(packed):
    high, low = split(packed)
    low = low.astype(f32)
    half, group = RANK // 2, lax.broadcasted_iota(jnp.int32, (RANK // 2, 128), 1) // RANK
    t1, t2 = low[RHS : RHS + half], roll(low[RHS + half : RHS + RANK], 32)
    r1, r2 = roll(low[RHS + RANK : ROWS - half], 32), roll(low[ROWS - half :], 64)
    fine = jnp.where(group == 0, t1, jnp.where(group == 1, t2, jnp.where(group == 2, r1, r2)))
    return jnp.concatenate([high, fine.astype(bf16)], axis=0)


def unpack(received):
    received = received.astype(f32)
    received, fine = received[:, :ROWS], received[:, ROWS:]
    own = received[:, RHS : RHS + RANK].reshape(WIDE, 128)
    cross = received[:, RHS + RANK :].reshape(WIDE, 128)
    lane_group = lax.broadcasted_iota(jnp.int32, (WIDE, 128), 1) // RANK

    def tiled(x, group):
        x = jnp.where(lane_group[: x.shape[0]] == group, x, 0.0)
        x = x + roll(x, 32)
        return x + roll(x, 64)

    half = RANK // 2
    low = [tiled(fine.reshape(FAN * half, 128), g).reshape(FAN, half, 128) for g in range(4)]
    t = tiled(own, 0) + jnp.concatenate(low[:2], axis=1).reshape(WIDE, 128)
    r = tiled(cross, 1) + jnp.concatenate(low[2:], axis=1).reshape(WIDE, 128)
    maps = (
        t,
        r,
        tiled(own, 1),
        tiled(own, 2),
        tiled(cross, 2),
        tiled(own, 3),
        tiled(cross, 3),
    )
    group = lax.broadcasted_iota(jnp.int32, (RHS, 128), 1) // RANK
    offsets = []
    for k in range(4):
        halves = []
        for half in range(2):
            out = jnp.zeros((RHS, 128), f32)
            for g in range(4):
                moved = roll(received[4 * half + g, :RHS], 32 * (g - k))
                out = jnp.where(group == g, moved, out)
            halves.append(out)
        offsets.append(jnp.concatenate(halves, axis=1))
    found = dict(zip(("o1", "o2", "o3", "o4"), offsets))
    found.update(zip(("T", "R", "A21", "A31", "A32", "A41", "A42"), maps))
    return found.get


def own_piece(entering, piece):
    rows = entering[-1].shape[0]
    col = lax.broadcasted_iota(jnp.int32, (rows, WIDE), 1) // RANK
    group = lax.broadcasted_iota(jnp.int32, (rows, 128), 1) // RANK
    out = jnp.zeros((rows, 128), f32)
    for k, e in enumerate(entering):
        if e.shape[0] < rows:
            e = jnp.concatenate([e, jnp.zeros((rows - e.shape[0], WIDE), f32)], axis=0)
        e = jnp.where(col == piece, e, 0.0)
        e = e[:, :128] + e[:, 128:]
        e = e + roll(e, 32)
        e = e + roll(e, 64)
        out = jnp.where(group == k, e, out)
    return out


def moved_on(x):
    return jnp.where(lax.broadcasted_iota(jnp.int32, x.shape, 1) >= 64, roll(x, 64), 0.0)


def pieces_kernel(
    ranks_any, v_any, li_any, ll_any, lr_any, ui_any, ul_any, ur_any,
    wire_out, entering_out, rows_out, data_out,
    ranks, v, li, ll, lr, ui, ul, ur, sems,
):
    copies = {}

    def start(name, source, target, at):
        copies[name] = pltpu.make_async_copy(source, target, sems.at[at])
        copies[name].start()

    start("v", v_any, v, 0)
    start("ll", ll_any, ll, 1)
    start("a", li_any, li, 6)
    start("ul", ul_any, ul, 2)
    start("b", ui_any, ui, 7)
    start("lr", lr_any, lr, 3)
    start("ur", ur_any, ur, 4)
    start("ranks", ranks_any, ranks, 5)

    group = lax.broadcasted_iota(jnp.int32, (RHS, 128), 1) // RANK
    eye = (
        lax.broadcasted_iota(jnp.int32, (RANK, 128), 0)
        == lax.broadcasted_iota(jnp.int32, (RANK, 128), 1) % RANK
    ).astype(f32)
    blocks = range(FAN)
    span = [slice(BS * i, BS * (i + 1)) for i in blocks]
    k = RHS + RANK
    va, c, d, m, n, vab, cb, last = ([None] * FAN for _ in range(8))
    kept = {name: [] for name in ("T", "R", "A21", "A31", "A32", "A41", "A42", "o1", "o2", "o3", "o4")}

    def masked(right, rank):
        keep = lax.broadcasted_iota(jnp.int32, (RANK, BS), 0) < rank
        w = jnp.where(keep, right.astype(f32), 0.0).astype(bf16)
        return jnp.concatenate([w] * 4, axis=0)

    for name in ("v", "ll", "a"):
        copies[name].wait()
    for i in blocks:
        one = dot_nt(jnp.concatenate([v[:, span[i]], ll[i]], axis=0), li[i])
        va[i] = one[:RHS]
        c[i] = (-one[RHS:]).astype(bf16)
    for name in ("ul", "b", "lr", "ur", "ranks"):
        copies[name].wait()

    def work():
        for i in blocks:
            two = dot_nt(jnp.concatenate([*split(va[i]), c[i], ul[i]], axis=0), ui[i])
            vab[i] = two[:RHS] + two[RHS : 2 * RHS]
            cb[i] = two[2 * RHS : 2 * RHS + RANK]
            d[i] = (-two[2 * RHS + RANK :]).astype(bf16)
            yield
            m[i], n[i] = masked(lr[i], ranks[0, i]), masked(ur[i], ranks[1, i])
            w = dot_nt(jnp.concatenate([c[i], *split(va[i])], axis=0), m[i])
            kept["T"].append(eye + w[:RANK])
            kept["o1"].append(w[RANK:k] + w[k:])
            yield
        for i in blocks:
            both = split(jnp.concatenate([vab[i], cb[i]], axis=0))
            three = dot_nt(jnp.concatenate([*both, d[i]], axis=0), li[i])
            last[i] = jnp.concatenate([three[:k] + three[k : 2 * k], three[2 * k :]], axis=0)
            yield
            w = dot_nt(jnp.concatenate([d[i], *split(jnp.concatenate([vab[i], cb[i]], axis=0))], axis=0), n[i])
            kept["R"].append(eye + w[:RANK])
            w = w[RANK : RANK + k] + w[RANK + k :]
            kept["o2"].append(w[:RHS])
            kept["A21"].append(w[RHS:])
            yield
        four = [None] * FAN
        for i in blocks:
            four[i] = wide_times_exact(last[i], ui[i], dot_nt)
            rows_out[:, span[i]] = jnp.concatenate([four[i][RHS:], cb[i], d[i].astype(f32)], axis=0)
            data_out[:, span[i]] = jnp.concatenate([vab[i], four[i][:RHS]], axis=0)
            yield
            w = wide_times_exact(last[i], m[i], dot_nt)
            kept["o3"].append(w[:RHS])
            kept["A31"].append(w[RHS:k])
            kept["A32"].append(w[k:])
            yield
        for i in blocks:
            w = wide_times_exact(four[i], n[i], dot_nt)
            kept["o4"].append(w[:RHS])
            kept["A41"].append(w[RHS:k])
            kept["A42"].append(w[k:])
            yield

    between = work()

    def get(name):
        while len(kept[name]) < FAN:
            next(between)
        if name[0] != "o":
            return jnp.concatenate(kept[name], axis=0)
        halves = []
        for half in (kept[name][:4], kept[name][4:]):
            out = half[0]
            for g in range(1, 4):
                out = jnp.where(group == g, half[g], out)
            halves.append(out)
        return jnp.concatenate(halves, axis=1)

    entering, packed = joined(get, True, False, between, 4)
    wire_out[...] = to_wire(packed)
    for j, e in enumerate(entering):
        entering_out[j, : e.shape[0]] = e
        if e.shape[0] < ROWS:
            entering_out[j, e.shape[0] :] = jnp.zeros((ROWS - e.shape[0], WIDE), f32)


def response_kernel(entering, rows, data, high_out, low_out, base_out):
    entering = [entering[j] for j in range(4)]
    for i in range(FAN):
        span = slice(BS * i, BS * (i + 1))
        s = own_piece(entering, i)
        both = jnp.concatenate([s, moved_on(s)], axis=0)
        y = times(both, split(rows[:, span]))
        base_out[:, span] = data[:, span] + jnp.concatenate(
            [y[ROWS : ROWS + RHS], y[:RHS]], axis=0
        )
        gain = split(jnp.concatenate([y[RHS:ROWS], y[ROWS + RHS :]], axis=0))
        high_out[:, span] = gain[0]
        low_out[:, span] = gain[1]


def device_gain(own):
    s1, s2 = own[RHS : RHS + RANK], own[RHS + RANK :]
    return jnp.concatenate([s1, s2, moved_on(s1), moved_on(s2)], axis=0)


def plane_kernel(place, *refs):
    *maps, wire_out, own_out, received = refs
    chip, core = place[0], place[1]
    for n, ref in enumerate(maps):
        far, other = n % 4, n // 4
        at = 2 * ((chip - far) % 4) + jnp.where(other == 1, 1 - core, core)
        received[at] = ref[...]
    entering, packed = joined(unpack(received[...]), True, True)
    wire = to_wire(packed)
    for e in range(FAN):
        wire_out[e] = wire
    own_out[...] = own_piece(entering, 2 * chip + core)


def outputs_kernel(place, received, own, high, low, base, first_out, second_out):
    entering, _ = joined(unpack(received[...]), False, True)
    plane = own_piece(entering, place[2])
    own = own[...]
    state = own[:RHS] + times(plane, split(device_gain(own)))
    both = jnp.concatenate([moved_on(state), state], axis=0)
    y = base[...] + times(both, (high[...], low[...]))
    first_out[...] = y[:RHS]
    second_out[...] = y[RHS:]


vmem = pl.BlockSpec(memory_space=pltpu.VMEM)
smem = pl.BlockSpec(memory_space=pltpu.SMEM)
hbm = pl.BlockSpec(memory_space=pltpu.HBM)


def call(kernel, name, out, specs, args, scratch=(), mib=16):
    return pl.pallas_call(
        kernel,
        out_shape=out,
        in_specs=specs,
        out_specs=jax.tree.map(lambda _: vmem, out),
        scratch_shapes=scratch,
        compiler_params=pltpu.CompilerParams(vmem_limit_bytes=mib << 20),
        name=name,
    )(*args)


def shape(*dims, dtype=f32):
    return jax.ShapeDtypeStruct(dims, dtype)


def local(
    right_sides, lower_inverse, lower_left, lower_right, upper_inverse, upper_left, upper_right, block_ranks
):
    order = right_sides.shape[1]
    index = lax.axis_index("rows")
    chip, core, plane = index % FAN // 2, index % 2, index // FAN
    place = jnp.stack([chip, core, plane]).astype(jnp.int32)
    n = lax.axis_size("rows")
    across = [[p * FAN + d for p in range(n // FAN)] for d in range(FAN)]
    to_core = [(i, i ^ 1) for i in range(n)]

    def along_y(far):
        return [(i, i // FAN * FAN + (i + 2 * far) % FAN) for i in range(n)]

    turned = [
        jnp.swapaxes(w, 1, 2) for w in (lower_left, lower_right, upper_left, upper_right)
    ]
    thin = pltpu.VMEM((FAN, RANK, BS), bf16)
    square = pltpu.VMEM((FAN, BS, BS), bf16)
    wire, entering, rows, data = call(
        pieces_kernel,
        "pieces",
        (
            shape(WIRE, 128, dtype=bf16),
            shape(4, ROWS, WIDE),
            shape(4 * RANK, order),
            shape(2 * RHS, order),
        ),
        [hbm] * 8,
        [
            pltpu.with_memory_space_constraint(x, pltpu.HBM)
            for x in (
                block_ranks, right_sides, lower_inverse, *turned[:2], upper_inverse, *turned[2:]
            )
        ],
        [
            pltpu.SMEM(block_ranks.shape, jnp.int32), pltpu.VMEM((RHS, order), bf16), square, thin, thin, square, thin, thin,
            pltpu.SemaphoreType.DMA((8,)),
        ],
    )
    chips = [wire] + [lax.ppermute(wire, "rows", along_y(far)) for far in (1, 2, 3)]
    high, low, base = call(
        response_kernel,
        "response",
        (shape(4 * RANK, order, dtype=bf16), shape(4 * RANK, order, dtype=bf16), shape(2 * RHS, order)),
        [vmem] * 3,
        (entering, rows, data),
    )
    chips[2], high, low, base = lax.optimization_barrier((chips[2], high, low, base))
    others = [lax.ppermute(x, "rows", to_core) for x in chips]
    wire, own = call(
        plane_kernel,
        "plane",
        (shape(FAN, WIRE, 128, dtype=bf16), shape(ROWS, 128)),
        [smem] + [vmem] * 8,
        (place, *chips, *others),
        [pltpu.VMEM((FAN, WIRE, 128), bf16)],
    )
    received = lax.all_to_all(wire, "rows", 0, 0, tiled=True, axis_index_groups=across)
    return call(
        outputs_kernel,
        "outputs",
        (shape(RHS, order), shape(RHS, order)),
        [smem] + [vmem] * 5,
        (place, received, own, high, low, base),
    )


def solution(mesh):
    placed_in = (
        P("rhs", "rows"),
        P("rows", None, None),
        P("rows", None, None),
        P("rows", None, None),
        P("rows", None, None),
        P("rows", None, None),
        P("rows", None, None),
        P(None, "rows"),
    )
    return jax.shard_map(
        local,
        mesh=mesh,
        in_specs=placed_in,
        out_specs=(P("rhs", "rows"), P("rhs", "rows")),
        check_vma=False,
    )
```

```python
import functools

import jax
import jax.numpy as jnp
from jax import lax
from jax.experimental import pallas as pl
from jax.experimental.pallas import tpu as pltpu
from jax.sharding import PartitionSpec as P

f32, bf16 = jnp.float32, jnp.bfloat16

BS = 256
RANK = 32
RHS = 16
FAN = 8
WIDE = FAN * RANK
ROWS = RHS + 2 * RANK
WIRE = ROWS + RANK // 2


def roll(x, shift):
    shift %= x.shape[1]
    return pltpu.roll(x, shift, 1) if shift else x


def split(x):
    high = x.astype(bf16)
    return high, (x - high.astype(f32)).astype(bf16)


def dot_nn(x, w):
    return lax.dot_general(x, w, (((1,), (0,)), ((), ())), preferred_element_type=f32)


def dot_nt(x, w):
    return lax.dot_general(x, w, (((1,), (1,)), ((), ())), preferred_element_type=f32)


def wide_times_exact(x, w, dot):
    n = x.shape[0]
    both = dot(jnp.concatenate(split(x), axis=0), w)
    return both[:n] + both[n:]


def stacked(x):
    high, low = split(x)
    return jnp.concatenate([high, low], axis=0), high


def times_parts(x, w):
    n = x[1].shape[0]
    both = dot_nn(x[0], w[0])
    out = both[:n] + both[n:]
    return out if w[1] is None else out + dot_nn(x[1], w[1])


def times(x, w):
    return times_parts(stacked(x), w)


def block_ids(shape):
    return (
        lax.broadcasted_iota(jnp.int32, shape, 0) // RANK,
        lax.broadcasted_iota(jnp.int32, shape, 1) // RANK,
    )


def placed(tiled, offset):
    tiled = jnp.concatenate([tiled, tiled], axis=1)
    row, col = block_ids(tiled.shape)
    return jnp.where(col == row + offset, tiled, 0.0)


def below(x, rows):
    return jnp.concatenate([x, jnp.zeros((rows - x.shape[0], x.shape[1]), x.dtype)], axis=0)


def above(x, rows):
    return jnp.concatenate([jnp.zeros((rows - x.shape[0], x.shape[1]), x.dtype), x], axis=0)


def joining(get, outward, exact):
    as_parts = (lambda w: (w.astype(bf16), None)) if exact else split
    one = (
        lax.broadcasted_iota(jnp.int32, (WIDE, WIDE), 0)
        == lax.broadcasted_iota(jnp.int32, (WIDE, WIDE), 1)
    ).astype(f32)
    sides = ((below, lambda x, n: x[: WIDE - n * RANK]), (above, lambda x, n: x[n * RANK :]))
    t, r = get("T"), get("R")
    hops = [placed(t, 1), placed(r, -1)]
    parts = [split(hop) for hop in hops]
    twos = [fill(times(cut(hop, 2), p), WIDE) for hop, p, (fill, cut) in zip(hops, parts, sides)]
    yield
    parts = [split(two) for two in twos]
    fours = [fill(times(cut(two, 4), p), WIDE) for two, p, (fill, cut) in zip(twos, parts, sides)]
    threes = [fill(times(cut(hop, 3), p), WIDE) for hop, p, (fill, cut) in zip(hops, parts, sides)]
    yield
    up, down = (
        near + fill(times(cut(near, 4), split(four)), WIDE)
        for near, four, (fill, cut) in zip(
            [one + hop + two + three for hop, two, three in zip(hops, twos, threes)], fours, sides
        )
    )
    yield
    gap = jnp.zeros((RANK, WIDE), f32)
    up_next = split(jnp.concatenate([up[RANK:], gap], axis=0))
    down_next = split(jnp.concatenate([gap, down[:-RANK]], axis=0))

    def with_rows(x, rows):
        return below(x, rows) if outward and x.shape[0] < rows else x

    e1 = times(get("o1"), up_next)
    d21 = as_parts(placed(get("A21"), 0))
    yield
    if outward:
        e1 = jnp.concatenate([e1, up[:RANK]], axis=0)
        dt, dr = split(placed(t, 0)), split(placed(r, 0))
    e1_parts = stacked(e1)
    q2 = with_rows(get("o2"), RHS + RANK) + times_parts(e1_parts, d21)
    yield
    e2 = times(q2, down_next)
    yield
    g31 = times_parts(e1_parts, as_parts(placed(get("A31"), 0)))
    if outward:
        g1 = times_parts(e1_parts, dt)
        e2 = jnp.concatenate([e2, down[-RANK:]], axis=0)
    e2_parts = stacked(e2)
    g32 = times_parts(e2_parts, as_parts(placed(get("A32"), 0)))
    yield
    q3 = with_rows(get("o3"), ROWS) + with_rows(g31, ROWS) + g32
    e3 = times(q3, up_next)
    yield
    g41 = times_parts(e1_parts, as_parts(placed(get("A41"), 0)))
    g42 = times_parts(e2_parts, as_parts(placed(get("A42"), 0)))
    if outward:
        g2 = times_parts(e2_parts, dr)
    e3_parts = stacked(e3)
    q4 = with_rows(get("o4"), ROWS) + with_rows(g41, ROWS) + g42 + times_parts(e3_parts, d21)
    yield
    e4 = times(q4, down_next)
    entering = (e1, e2, e3, e4)
    if not outward:
        return entering, None
    g3 = times_parts(e3_parts, dt)
    g4 = times(e4, dr)
    last, first = slice(128, 256), slice(0, 128)
    group = lax.broadcasted_iota(jnp.int32, (ROWS, 128), 1) // RANK
    t1 = roll(with_rows(with_rows(get("o1"), RHS + RANK) + g1, ROWS)[:, last], 32)
    t2 = roll((with_rows(q2, ROWS) + g2)[:, first], 32)
    t3 = roll((q3 + g3)[:, last], 96)
    t4 = roll((q4 + g4)[:, first], 96)
    packed = jnp.where(
        group == 0, t1, jnp.where(group == 1, t2, jnp.where(group == 2, t3, t4))
    )
    return entering, packed


def joined(parts, outward, exact, between=iter(()), every=0):
    steps = joining(parts, outward, exact)
    while True:
        try:
            next(steps)
        except StopIteration as end:
            return end.value
        for _ in range(every):
            next(between, None)


def to_wire(packed):
    high, low = split(packed)
    low = low.astype(f32)
    half, group = RANK // 2, lax.broadcasted_iota(jnp.int32, (RANK // 2, 128), 1) // RANK
    t1, t2 = low[RHS : RHS + half], roll(low[RHS + half : RHS + RANK], 32)
    r1, r2 = roll(low[RHS + RANK : ROWS - half], 32), roll(low[ROWS - half :], 64)
    fine = jnp.where(group == 0, t1, jnp.where(group == 1, t2, jnp.where(group == 2, r1, r2)))
    return jnp.concatenate([high, fine.astype(bf16)], axis=0)


def unpack(received):
    received = received.astype(f32)
    received, fine = received[:, :ROWS], received[:, ROWS:]
    own = received[:, RHS : RHS + RANK].reshape(WIDE, 128)
    cross = received[:, RHS + RANK :].reshape(WIDE, 128)
    lane_group = lax.broadcasted_iota(jnp.int32, (WIDE, 128), 1) // RANK

    def tiled(x, group):
        x = jnp.where(lane_group[: x.shape[0]] == group, x, 0.0)
        x = x + roll(x, 32)
        return x + roll(x, 64)

    half = RANK // 2
    low = [tiled(fine.reshape(FAN * half, 128), g).reshape(FAN, half, 128) for g in range(4)]
    t = tiled(own, 0) + jnp.concatenate(low[:2], axis=1).reshape(WIDE, 128)
    r = tiled(cross, 1) + jnp.concatenate(low[2:], axis=1).reshape(WIDE, 128)
    maps = (
        t,
        r,
        tiled(own, 1),
        tiled(own, 2),
        tiled(cross, 2),
        tiled(own, 3),
        tiled(cross, 3),
    )
    group = lax.broadcasted_iota(jnp.int32, (RHS, 128), 1) // RANK
    offsets = []
    for k in range(4):
        halves = []
        for half in range(2):
            out = jnp.zeros((RHS, 128), f32)
            for g in range(4):
                moved = roll(received[4 * half + g, :RHS], 32 * (g - k))
                out = jnp.where(group == g, moved, out)
            halves.append(out)
        offsets.append(jnp.concatenate(halves, axis=1))
    found = dict(zip(("o1", "o2", "o3", "o4"), offsets))
    found.update(zip(("T", "R", "A21", "A31", "A32", "A41", "A42"), maps))
    return found.get


def own_piece(entering, piece):
    rows = entering[-1].shape[0]
    col = lax.broadcasted_iota(jnp.int32, (rows, WIDE), 1) // RANK
    group = lax.broadcasted_iota(jnp.int32, (rows, 128), 1) // RANK
    out = jnp.zeros((rows, 128), f32)
    for k, e in enumerate(entering):
        if e.shape[0] < rows:
            e = jnp.concatenate([e, jnp.zeros((rows - e.shape[0], WIDE), f32)], axis=0)
        e = jnp.where(col == piece, e, 0.0)
        e = e[:, :128] + e[:, 128:]
        e = e + roll(e, 32)
        e = e + roll(e, 64)
        out = jnp.where(group == k, e, out)
    return out


def place():
    index = lax.axis_index("rows")
    return lax.rem(index, FAN) // 2, lax.rem(index, 2), index // FAN


def moved_on(x):
    return jnp.where(lax.broadcasted_iota(jnp.int32, x.shape, 1) >= 64, roll(x, 64), 0.0)


def pieces_kernel(
    ranks_any, v_any, li_any, ll_any, lr_any, ui_any, ul_any, ur_any,
    wire_out, entering_out, rows_out, data_out,
    ranks, v, li, ll, lr, ui, ul, ur, sems,
):
    copies = {}

    def start(name, source, target, at):
        copies[name] = pltpu.make_async_copy(source, target, sems.at[at])
        copies[name].start()

    start("v", v_any, v, 0)
    start("ll", ll_any, ll, 1)
    start("a", li_any, li, 6)
    start("ul", ul_any, ul, 2)
    start("b", ui_any, ui, 7)
    start("lr", lr_any, lr, 3)
    start("ur", ur_any, ur, 4)
    start("ranks", ranks_any, ranks, 5)

    group = lax.broadcasted_iota(jnp.int32, (RHS, 128), 1) // RANK
    eye = (
        lax.broadcasted_iota(jnp.int32, (RANK, 128), 0)
        == lax.broadcasted_iota(jnp.int32, (RANK, 128), 1) % RANK
    ).astype(f32)
    blocks = range(FAN)
    span = [slice(BS * i, BS * (i + 1)) for i in blocks]
    k = RHS + RANK
    va, c, d, m, n, vab, cb, last = ([None] * FAN for _ in range(8))
    kept = {name: [] for name in ("T", "R", "A21", "A31", "A32", "A41", "A42", "o1", "o2", "o3", "o4")}

    def masked(right, rank):
        keep = lax.broadcasted_iota(jnp.int32, (RANK, BS), 0) < rank
        w = jnp.where(keep, right.astype(f32), 0.0).astype(bf16)
        return jnp.concatenate([w] * 4, axis=0)

    for name in ("v", "ll", "a"):
        copies[name].wait()
    for i in blocks:
        one = dot_nt(jnp.concatenate([v[:, span[i]], ll[i]], axis=0), li[i])
        va[i] = one[:RHS]
        c[i] = (-one[RHS:]).astype(bf16)
    for name in ("ul", "b", "lr", "ur", "ranks"):
        copies[name].wait()

    def work():
        for i in blocks:
            two = dot_nt(jnp.concatenate([*split(va[i]), c[i], ul[i]], axis=0), ui[i])
            vab[i] = two[:RHS] + two[RHS : 2 * RHS]
            cb[i] = two[2 * RHS : 2 * RHS + RANK]
            d[i] = (-two[2 * RHS + RANK :]).astype(bf16)
            yield
            m[i], n[i] = masked(lr[i], ranks[0, i]), masked(ur[i], ranks[1, i])
            w = dot_nt(jnp.concatenate([c[i], *split(va[i])], axis=0), m[i])
            kept["T"].append(eye + w[:RANK])
            kept["o1"].append(w[RANK:k] + w[k:])
            yield
        for i in blocks:
            both = split(jnp.concatenate([vab[i], cb[i]], axis=0))
            three = dot_nt(jnp.concatenate([*both, d[i]], axis=0), li[i])
            last[i] = jnp.concatenate([three[:k] + three[k : 2 * k], three[2 * k :]], axis=0)
            yield
            w = dot_nt(jnp.concatenate([d[i], *split(jnp.concatenate([vab[i], cb[i]], axis=0))], axis=0), n[i])
            kept["R"].append(eye + w[:RANK])
            w = w[RANK : RANK + k] + w[RANK + k :]
            kept["o2"].append(w[:RHS])
            kept["A21"].append(w[RHS:])
            yield
        four = [None] * FAN
        for i in blocks:
            four[i] = wide_times_exact(last[i], ui[i], dot_nt)
            rows_out[:, span[i]] = jnp.concatenate([four[i][RHS:], cb[i], d[i].astype(f32)], axis=0)
            data_out[:, span[i]] = jnp.concatenate([vab[i], four[i][:RHS]], axis=0)
            yield
            w = wide_times_exact(last[i], m[i], dot_nt)
            kept["o3"].append(w[:RHS])
            kept["A31"].append(w[RHS:k])
            kept["A32"].append(w[k:])
            yield
        for i in blocks:
            w = wide_times_exact(four[i], n[i], dot_nt)
            kept["o4"].append(w[:RHS])
            kept["A41"].append(w[RHS:k])
            kept["A42"].append(w[k:])
            yield

    between = work()

    def get(name):
        while len(kept[name]) < FAN:
            next(between)
        if name[0] != "o":
            return jnp.concatenate(kept[name], axis=0)
        halves = []
        for half in (kept[name][:4], kept[name][4:]):
            out = half[0]
            for g in range(1, 4):
                out = jnp.where(group == g, half[g], out)
            halves.append(out)
        return jnp.concatenate(halves, axis=1)

    entering, packed = joined(get, True, False, between, 4)
    wire_out[...] = to_wire(packed)
    for j, e in enumerate(entering):
        entering_out[j, : e.shape[0]] = e
        if e.shape[0] < ROWS:
            entering_out[j, e.shape[0] :] = jnp.zeros((ROWS - e.shape[0], WIDE), f32)


def response_kernel(entering, rows, data, high_out, low_out, base_out):
    entering = [entering[j] for j in range(4)]
    for i in range(FAN):
        span = slice(BS * i, BS * (i + 1))
        s = own_piece(entering, i)
        both = jnp.concatenate([s, moved_on(s)], axis=0)
        y = times(both, split(rows[:, span]))
        base_out[:, span] = data[:, span] + jnp.concatenate(
            [y[ROWS : ROWS + RHS], y[:RHS]], axis=0
        )
        gain = split(jnp.concatenate([y[RHS:ROWS], y[ROWS + RHS :]], axis=0))
        high_out[:, span] = gain[0]
        low_out[:, span] = gain[1]


def device_gain(own):
    s1, s2 = own[RHS : RHS + RANK], own[RHS + RANK :]
    return jnp.concatenate([s1, s2, moved_on(s1), moved_on(s2)], axis=0)


def plane_kernel(*refs):
    *maps, wire_out, own_out, received = refs
    chip, core, _ = place()
    for n, ref in enumerate(maps):
        far, other = n % 4, n // 4
        at = 2 * ((chip - far) % 4) + jnp.where(other == 1, 1 - core, core)
        received[at] = ref[...]
    entering, packed = joined(unpack(received[...]), True, True)
    wire = to_wire(packed)
    for e in range(FAN):
        wire_out[e] = wire
    own_out[...] = own_piece(entering, 2 * chip + core)


def outputs_kernel(received, own, high, low, base, first_out, second_out):
    entering, _ = joined(unpack(received[...]), False, True)
    plane = own_piece(entering, place()[2])
    own = own[...]
    state = own[:RHS] + times(plane, split(device_gain(own)))
    both = jnp.concatenate([moved_on(state), state], axis=0)
    y = base[...] + times(both, (high[...], low[...]))
    first_out[...] = y[:RHS]
    second_out[...] = y[RHS:]


vmem = pl.BlockSpec(memory_space=pltpu.VMEM)
hbm = pl.BlockSpec(memory_space=pltpu.HBM)


def call(kernel, name, out, specs, args, scratch=(), mib=16):
    return pl.pallas_call(
        kernel,
        out_shape=out,
        in_specs=specs,
        out_specs=jax.tree.map(lambda _: vmem, out),
        scratch_shapes=scratch,
        compiler_params=pltpu.CompilerParams(vmem_limit_bytes=mib << 20),
        name=name,
    )(*args)


def shape(*dims, dtype=f32):
    return jax.ShapeDtypeStruct(dims, dtype)


def local(
    right_sides, lower_inverse, lower_left, lower_right, upper_inverse, upper_left, upper_right, block_ranks
):
    order = right_sides.shape[1]
    n = lax.axis_size("rows")
    across = [[p * FAN + d for p in range(n // FAN)] for d in range(FAN)]
    to_core = [(i, i ^ 1) for i in range(n)]

    def along_y(far):
        return [(i, i // FAN * FAN + (i + 2 * far) % FAN) for i in range(n)]

    turned = [
        jnp.swapaxes(w, 1, 2) for w in (lower_left, lower_right, upper_left, upper_right)
    ]
    thin = pltpu.VMEM((FAN, RANK, BS), bf16)
    square = pltpu.VMEM((FAN, BS, BS), bf16)
    wire, entering, rows, data = call(
        pieces_kernel,
        "pieces",
        (
            shape(WIRE, 128, dtype=bf16),
            shape(4, ROWS, WIDE),
            shape(4 * RANK, order),
            shape(2 * RHS, order),
        ),
        [hbm] * 8,
        [
            pltpu.with_memory_space_constraint(x, pltpu.HBM)
            for x in (
                block_ranks, right_sides, lower_inverse, *turned[:2], upper_inverse, *turned[2:]
            )
        ],
        [
            pltpu.SMEM(block_ranks.shape, jnp.int32), pltpu.VMEM((RHS, order), bf16), square, thin, thin, square, thin, thin,
            pltpu.SemaphoreType.DMA((8,)),
        ],
    )
    chips = [wire] + [lax.ppermute(wire, "rows", along_y(far)) for far in (1, 2, 3)]
    high, low, base = call(
        response_kernel,
        "response",
        (shape(4 * RANK, order, dtype=bf16), shape(4 * RANK, order, dtype=bf16), shape(2 * RHS, order)),
        [vmem] * 3,
        (entering, rows, data),
    )
    chips[2], high, low, base = lax.optimization_barrier((chips[2], high, low, base))
    others = [lax.ppermute(x, "rows", to_core) for x in chips]
    wire, own = call(
        plane_kernel,
        "plane",
        (shape(FAN, WIRE, 128, dtype=bf16), shape(ROWS, 128)),
        [vmem] * 8,
        (*chips, *others),
        [pltpu.VMEM((FAN, WIRE, 128), bf16)],
    )
    received = lax.all_to_all(wire, "rows", 0, 0, tiled=True, axis_index_groups=across)
    return call(
        outputs_kernel,
        "outputs",
        (shape(RHS, order), shape(RHS, order)),
        [vmem] * 5,
        (received, own, high, low, base),
    )


def solution(mesh):
    placed_in = (
        P("rhs", "rows"),
        P("rows", None, None),
        P("rows", None, None),
        P("rows", None, None),
        P("rows", None, None),
        P("rows", None, None),
        P("rows", None, None),
        P(None, "rows"),
    )
    return jax.shard_map(
        local,
        mesh=mesh,
        in_specs=placed_in,
        out_specs=(P("rhs", "rows"), P("rhs", "rows")),
        check_vma=False,
    )
```

```python
import functools

import jax
import jax.numpy as jnp
from jax import lax
from jax.experimental import pallas as pl
from jax.experimental.pallas import tpu as pltpu
from jax.sharding import PartitionSpec as P

f32, bf16 = jnp.float32, jnp.bfloat16

BS = 256
RANK = 32
RHS = 16
FAN = 8
WIDE = FAN * RANK
ROWS = RHS + 2 * RANK
WIRE = ROWS + RANK // 2


def roll(x, shift):
    shift %= x.shape[1]
    return pltpu.roll(x, shift, 1) if shift else x


def split(x):
    high = x.astype(bf16)
    return high, (x - high.astype(f32)).astype(bf16)


def dot_nn(x, w):
    return lax.dot_general(x, w, (((1,), (0,)), ((), ())), preferred_element_type=f32)


def dot_nt(x, w):
    return lax.dot_general(x, w, (((1,), (1,)), ((), ())), preferred_element_type=f32)


def wide_times_exact(x, w, dot):
    n = x.shape[0]
    both = dot(jnp.concatenate(split(x), axis=0), w)
    return both[:n] + both[n:]


def stacked(x):
    high, low = split(x)
    return jnp.concatenate([high, low], axis=0), high


def times_parts(x, w):
    n = x[1].shape[0]
    both = dot_nn(x[0], w[0])
    out = both[:n] + both[n:]
    return out if w[1] is None else out + dot_nn(x[1], w[1])


def times(x, w):
    return times_parts(stacked(x), w)


def block_ids(shape):
    return (
        lax.broadcasted_iota(jnp.int32, shape, 0) // RANK,
        lax.broadcasted_iota(jnp.int32, shape, 1) // RANK,
    )


def placed(tiled, offset):
    tiled = jnp.concatenate([tiled, tiled], axis=1)
    row, col = block_ids(tiled.shape)
    return jnp.where(col == row + offset, tiled, 0.0)


def below(x, rows):
    return jnp.concatenate([x, jnp.zeros((rows - x.shape[0], x.shape[1]), x.dtype)], axis=0)


def above(x, rows):
    return jnp.concatenate([jnp.zeros((rows - x.shape[0], x.shape[1]), x.dtype), x], axis=0)


def joining(get, outward, exact):
    as_parts = (lambda w: (w.astype(bf16), None)) if exact else split
    one = (
        lax.broadcasted_iota(jnp.int32, (WIDE, WIDE), 0)
        == lax.broadcasted_iota(jnp.int32, (WIDE, WIDE), 1)
    ).astype(f32)
    sides = ((below, lambda x, n: x[: WIDE - n * RANK]), (above, lambda x, n: x[n * RANK :]))
    t, r = get("T"), get("R")
    hops = [placed(t, 1), placed(r, -1)]
    parts = [split(hop) for hop in hops]
    twos = [fill(times(cut(hop, 2), p), WIDE) for hop, p, (fill, cut) in zip(hops, parts, sides)]
    yield
    parts = [split(two) for two in twos]
    fours = [fill(times(cut(two, 4), p), WIDE) for two, p, (fill, cut) in zip(twos, parts, sides)]
    threes = [fill(times(cut(hop, 3), p), WIDE) for hop, p, (fill, cut) in zip(hops, parts, sides)]
    yield
    up, down = (
        near + fill(times(cut(near, 4), split(four)), WIDE)
        for near, four, (fill, cut) in zip(
            [one + hop + two + three for hop, two, three in zip(hops, twos, threes)], fours, sides
        )
    )
    yield
    gap = jnp.zeros((RANK, WIDE), f32)
    up_next = split(jnp.concatenate([up[RANK:], gap], axis=0))
    down_next = split(jnp.concatenate([gap, down[:-RANK]], axis=0))

    def with_rows(x, rows):
        return below(x, rows) if outward and x.shape[0] < rows else x

    e1 = times(get("o1"), up_next)
    d21 = as_parts(placed(get("A21"), 0))
    yield
    if outward:
        e1 = jnp.concatenate([e1, up[:RANK]], axis=0)
        dt, dr = split(placed(t, 0)), split(placed(r, 0))
    e1_parts = stacked(e1)
    q2 = with_rows(get("o2"), RHS + RANK) + times_parts(e1_parts, d21)
    yield
    e2 = times(q2, down_next)
    yield
    g31 = times_parts(e1_parts, as_parts(placed(get("A31"), 0)))
    if outward:
        g1 = times_parts(e1_parts, dt)
        e2 = jnp.concatenate([e2, down[-RANK:]], axis=0)
    e2_parts = stacked(e2)
    g32 = times_parts(e2_parts, as_parts(placed(get("A32"), 0)))
    yield
    q3 = with_rows(get("o3"), ROWS) + with_rows(g31, ROWS) + g32
    e3 = times(q3, up_next)
    yield
    g41 = times_parts(e1_parts, as_parts(placed(get("A41"), 0)))
    g42 = times_parts(e2_parts, as_parts(placed(get("A42"), 0)))
    if outward:
        g2 = times_parts(e2_parts, dr)
    e3_parts = stacked(e3)
    q4 = with_rows(get("o4"), ROWS) + with_rows(g41, ROWS) + g42 + times_parts(e3_parts, d21)
    yield
    e4 = times(q4, down_next)
    entering = (e1, e2, e3, e4)
    if not outward:
        return entering, None
    g3 = times_parts(e3_parts, dt)
    g4 = times(e4, dr)
    last, first = slice(128, 256), slice(0, 128)
    group = lax.broadcasted_iota(jnp.int32, (ROWS, 128), 1) // RANK
    t1 = roll(with_rows(with_rows(get("o1"), RHS + RANK) + g1, ROWS)[:, last], 32)
    t2 = roll((with_rows(q2, ROWS) + g2)[:, first], 32)
    t3 = roll((q3 + g3)[:, last], 96)
    t4 = roll((q4 + g4)[:, first], 96)
    packed = jnp.where(
        group == 0, t1, jnp.where(group == 1, t2, jnp.where(group == 2, t3, t4))
    )
    return entering, packed


def joined(parts, outward, exact, between=iter(()), every=0):
    steps = joining(parts, outward, exact)
    while True:
        try:
            next(steps)
        except StopIteration as end:
            return end.value
        for _ in range(every):
            next(between, None)


def to_wire(packed):
    high, low = split(packed)
    low = low.astype(f32)
    half, group = RANK // 2, lax.broadcasted_iota(jnp.int32, (RANK // 2, 128), 1) // RANK
    t1, t2 = low[RHS : RHS + half], roll(low[RHS + half : RHS + RANK], 32)
    r1, r2 = roll(low[RHS + RANK : ROWS - half], 32), roll(low[ROWS - half :], 64)
    fine = jnp.where(group == 0, t1, jnp.where(group == 1, t2, jnp.where(group == 2, r1, r2)))
    return jnp.concatenate([high, fine.astype(bf16)], axis=0)


def unpack(received):
    received = received.astype(f32)
    received, fine = received[:, :ROWS], received[:, ROWS:]
    own = received[:, RHS : RHS + RANK].reshape(WIDE, 128)
    cross = received[:, RHS + RANK :].reshape(WIDE, 128)
    lane_group = lax.broadcasted_iota(jnp.int32, (WIDE, 128), 1) // RANK

    def tiled(x, group):
        x = jnp.where(lane_group[: x.shape[0]] == group, x, 0.0)
        x = x + roll(x, 32)
        return x + roll(x, 64)

    half = RANK // 2
    low = [tiled(fine.reshape(FAN * half, 128), g).reshape(FAN, half, 128) for g in range(4)]
    t = tiled(own, 0) + jnp.concatenate(low[:2], axis=1).reshape(WIDE, 128)
    r = tiled(cross, 1) + jnp.concatenate(low[2:], axis=1).reshape(WIDE, 128)
    maps = (
        t,
        r,
        tiled(own, 1),
        tiled(own, 2),
        tiled(cross, 2),
        tiled(own, 3),
        tiled(cross, 3),
    )
    group = lax.broadcasted_iota(jnp.int32, (RHS, 128), 1) // RANK
    offsets = []
    for k in range(4):
        halves = []
        for half in range(2):
            out = jnp.zeros((RHS, 128), f32)
            for g in range(4):
                moved = roll(received[4 * half + g, :RHS], 32 * (g - k))
                out = jnp.where(group == g, moved, out)
            halves.append(out)
        offsets.append(jnp.concatenate(halves, axis=1))
    found = dict(zip(("o1", "o2", "o3", "o4"), offsets))
    found.update(zip(("T", "R", "A21", "A31", "A32", "A41", "A42"), maps))
    return found.get


def own_piece(entering, piece):
    rows = entering[-1].shape[0]
    col = lax.broadcasted_iota(jnp.int32, (rows, WIDE), 1) // RANK
    group = lax.broadcasted_iota(jnp.int32, (rows, 128), 1) // RANK
    out = jnp.zeros((rows, 128), f32)
    for k, e in enumerate(entering):
        if e.shape[0] < rows:
            e = jnp.concatenate([e, jnp.zeros((rows - e.shape[0], WIDE), f32)], axis=0)
        e = jnp.where(col == piece, e, 0.0)
        e = e[:, :128] + e[:, 128:]
        e = e + roll(e, 32)
        e = e + roll(e, 64)
        out = jnp.where(group == k, e, out)
    return out


def place():
    index = lax.axis_index("rows")
    return lax.rem(index, FAN) // 2, lax.rem(index, 2), index // FAN


def moved_on(x):
    return jnp.where(lax.broadcasted_iota(jnp.int32, x.shape, 1) >= 64, roll(x, 64), 0.0)


def pieces_kernel(
    ranks_any, v_any, li_any, ll_any, lr_any, ui_any, ul_any, ur_any,
    wire_out, entering_out, rows_out, data_out,
    ranks, v, li, ll, lr, ui, ul, ur, sems,
):
    copies = {}

    def start(name, source, target, at):
        copies[name] = pltpu.make_async_copy(source, target, sems.at[at])
        copies[name].start()

    start("v", v_any, v, 0)
    start("ll", ll_any, ll, 1)
    start("a", li_any, li, 6)
    start("ul", ul_any, ul, 2)
    start("b", ui_any, ui, 7)
    start("lr", lr_any, lr, 3)
    start("ur", ur_any, ur, 4)
    start("ranks", ranks_any, ranks, 5)

    group = lax.broadcasted_iota(jnp.int32, (RHS, 128), 1) // RANK
    eye = (
        lax.broadcasted_iota(jnp.int32, (RANK, 128), 0)
        == lax.broadcasted_iota(jnp.int32, (RANK, 128), 1) % RANK
    ).astype(f32)
    blocks = range(FAN)
    span = [slice(BS * i, BS * (i + 1)) for i in blocks]
    k = RHS + RANK
    va, c, d, m, n, vab, cb, last = ([None] * FAN for _ in range(8))
    kept = {name: [] for name in ("T", "R", "A21", "A31", "A32", "A41", "A42", "o1", "o2", "o3", "o4")}

    def masked(right, rank):
        keep = lax.broadcasted_iota(jnp.int32, (RANK, BS), 0) < rank
        w = jnp.where(keep, right.astype(f32), 0.0).astype(bf16)
        return jnp.concatenate([w] * 4, axis=0)

    for name in ("v", "ll", "a"):
        copies[name].wait()
    for i in blocks:
        one = dot_nt(jnp.concatenate([v[:, span[i]], ll[i]], axis=0), li[i])
        va[i] = one[:RHS]
        c[i] = (-one[RHS:]).astype(bf16)
    for name in ("ul", "b", "lr", "ur", "ranks"):
        copies[name].wait()

    def work():
        for i in blocks:
            two = dot_nt(jnp.concatenate([*split(va[i]), c[i], ul[i]], axis=0), ui[i])
            vab[i] = two[:RHS] + two[RHS : 2 * RHS]
            cb[i] = two[2 * RHS : 2 * RHS + RANK]
            d[i] = (-two[2 * RHS + RANK :]).astype(bf16)
            yield
            m[i], n[i] = masked(lr[i], ranks[0, i]), masked(ur[i], ranks[1, i])
            w = dot_nt(jnp.concatenate([c[i], *split(va[i])], axis=0), m[i])
            kept["T"].append(eye + w[:RANK])
            kept["o1"].append(w[RANK:k] + w[k:])
            yield
        for i in blocks:
            both = split(jnp.concatenate([vab[i], cb[i]], axis=0))
            three = dot_nt(jnp.concatenate([*both, d[i]], axis=0), li[i])
            last[i] = jnp.concatenate([three[:k] + three[k : 2 * k], three[2 * k :]], axis=0)
            yield
            w = dot_nt(jnp.concatenate([d[i], *split(jnp.concatenate([vab[i], cb[i]], axis=0))], axis=0), n[i])
            kept["R"].append(eye + w[:RANK])
            w = w[RANK : RANK + k] + w[RANK + k :]
            kept["o2"].append(w[:RHS])
            kept["A21"].append(w[RHS:])
            yield
        four = [None] * FAN
        for i in blocks:
            four[i] = wide_times_exact(last[i], ui[i], dot_nt)
            rows_out[:, span[i]] = jnp.concatenate([four[i][RHS:], cb[i], d[i].astype(f32)], axis=0)
            data_out[:, span[i]] = jnp.concatenate([vab[i], four[i][:RHS]], axis=0)
            yield
            w = wide_times_exact(last[i], m[i], dot_nt)
            kept["o3"].append(w[:RHS])
            kept["A31"].append(w[RHS:k])
            kept["A32"].append(w[k:])
            yield
        for i in blocks:
            w = wide_times_exact(four[i], n[i], dot_nt)
            kept["o4"].append(w[:RHS])
            kept["A41"].append(w[RHS:k])
            kept["A42"].append(w[k:])
            yield

    between = work()

    def get(name):
        while len(kept[name]) < FAN:
            next(between)
        if name[0] != "o":
            return jnp.concatenate(kept[name], axis=0)
        halves = []
        for half in (kept[name][:4], kept[name][4:]):
            out = half[0]
            for g in range(1, 4):
                out = jnp.where(group == g, half[g], out)
            halves.append(out)
        return jnp.concatenate(halves, axis=1)

    entering, packed = joined(get, True, False, between, 4)
    wire_out[...] = to_wire(packed)
    for j, e in enumerate(entering):
        entering_out[j, : e.shape[0]] = e
        if e.shape[0] < ROWS:
            entering_out[j, e.shape[0] :] = jnp.zeros((ROWS - e.shape[0], WIDE), f32)


def response_kernel(entering, rows, data, high_out, low_out, base_out):
    entering = [entering[j] for j in range(4)]
    for i in range(FAN):
        span = slice(BS * i, BS * (i + 1))
        s = own_piece(entering, i)
        both = jnp.concatenate([s, moved_on(s)], axis=0)
        y = times(both, split(rows[:, span]))
        base_out[:, span] = data[:, span] + jnp.concatenate(
            [y[ROWS : ROWS + RHS], y[:RHS]], axis=0
        )
        gain = split(jnp.concatenate([y[RHS:ROWS], y[ROWS + RHS :]], axis=0))
        high_out[:, span] = gain[0]
        low_out[:, span] = gain[1]


def device_gain(own):
    s1, s2 = own[RHS : RHS + RANK], own[RHS + RANK :]
    return jnp.concatenate([s1, s2, moved_on(s1), moved_on(s2)], axis=0)


def plane_kernel(*refs):
    *pairs, wire_out, own_out, received = refs
    chip, core, _ = place()
    for far, pair in enumerate(pairs):
        at = 2 * lax.rem(chip + 4 - far, 4)
        received[at + core] = pair[0]
        received[at + 1 - core] = pair[1]
    entering, packed = joined(unpack(received[...]), True, True)
    wire = to_wire(packed)
    for e in range(FAN):
        wire_out[e] = wire
    own_out[...] = own_piece(entering, 2 * chip + core)


def outputs_kernel(received, own, high, low, base, first_out, second_out):
    entering, _ = joined(unpack(received[...]), False, True)
    plane = own_piece(entering, place()[2])
    own = own[...]
    state = own[:RHS] + times(plane, split(device_gain(own)))
    both = jnp.concatenate([moved_on(state), state], axis=0)
    y = base[...] + times(both, (high[...], low[...]))
    first_out[...] = y[:RHS]
    second_out[...] = y[RHS:]


vmem = pl.BlockSpec(memory_space=pltpu.VMEM)
hbm = pl.BlockSpec(memory_space=pltpu.HBM)


def call(kernel, name, out, specs, args, scratch=(), mib=16):
    return pl.pallas_call(
        kernel,
        out_shape=out,
        in_specs=specs,
        out_specs=jax.tree.map(lambda _: vmem, out),
        scratch_shapes=scratch,
        compiler_params=pltpu.CompilerParams(vmem_limit_bytes=mib << 20),
        name=name,
    )(*args)


def shape(*dims, dtype=f32):
    return jax.ShapeDtypeStruct(dims, dtype)


def local(
    right_sides, lower_inverse, lower_left, lower_right, upper_inverse, upper_left, upper_right, block_ranks
):
    order = right_sides.shape[1]
    n = lax.axis_size("rows")
    across = [[p * FAN + d for p in range(n // FAN)] for d in range(FAN)]
    to_core = [(i, i ^ 1) for i in range(n)]

    def along_y(far):
        return [(i, i // FAN * FAN + (i + 2 * far) % FAN) for i in range(n)]

    turned = [
        jnp.swapaxes(w, 1, 2) for w in (lower_left, lower_right, upper_left, upper_right)
    ]
    thin = pltpu.VMEM((FAN, RANK, BS), bf16)
    square = pltpu.VMEM((FAN, BS, BS), bf16)
    wire, entering, rows, data = call(
        pieces_kernel,
        "pieces",
        (
            shape(WIRE, 128, dtype=bf16),
            shape(4, ROWS, WIDE),
            shape(4 * RANK, order),
            shape(2 * RHS, order),
        ),
        [hbm] * 8,
        [
            pltpu.with_memory_space_constraint(x, pltpu.HBM)
            for x in (
                block_ranks, right_sides, lower_inverse, *turned[:2], upper_inverse, *turned[2:]
            )
        ],
        [
            pltpu.SMEM(block_ranks.shape, jnp.int32), pltpu.VMEM((RHS, order), bf16), square, thin, thin, square, thin, thin,
            pltpu.SemaphoreType.DMA((8,)),
        ],
    )
    pair = jnp.stack([wire, lax.ppermute(wire, "rows", to_core)])
    chips = [pair] + [lax.ppermute(pair, "rows", along_y(far)) for far in (1, 2, 3)]
    high, low, base = call(
        response_kernel,
        "response",
        (shape(4 * RANK, order, dtype=bf16), shape(4 * RANK, order, dtype=bf16), shape(2 * RHS, order)),
        [vmem] * 3,
        (entering, rows, data),
    )
    chips[2], high, low, base = lax.optimization_barrier((chips[2], high, low, base))
    wire, own = call(
        plane_kernel,
        "plane",
        (shape(FAN, WIRE, 128, dtype=bf16), shape(ROWS, 128)),
        [vmem] * 4,
        chips,
        [pltpu.VMEM((FAN, WIRE, 128), bf16)],
    )
    received = lax.all_to_all(wire, "rows", 0, 0, tiled=True, axis_index_groups=across)
    return call(
        outputs_kernel,
        "outputs",
        (shape(RHS, order), shape(RHS, order)),
        [vmem] * 5,
        (received, own, high, low, base),
    )


def solution(mesh):
    placed_in = (
        P("rhs", "rows"),
        P("rows", None, None),
        P("rows", None, None),
        P("rows", None, None),
        P("rows", None, None),
        P("rows", None, None),
        P("rows", None, None),
        P(None, "rows"),
    )
    return jax.shard_map(
        local,
        mesh=mesh,
        in_specs=placed_in,
        out_specs=(P("rhs", "rows"), P("rhs", "rows")),
        check_vma=False,
    )
```

```python
import functools

import jax
import jax.numpy as jnp
from jax import lax
from jax.experimental import pallas as pl
from jax.experimental.pallas import tpu as pltpu
from jax.sharding import PartitionSpec as P

f32, bf16 = jnp.float32, jnp.bfloat16

BS = 256
RANK = 32
RHS = 16
FAN = 8
WIDE = FAN * RANK
ROWS = RHS + 2 * RANK
WIRE = ROWS + RANK // 2


def roll(x, shift):
    shift %= x.shape[1]
    return pltpu.roll(x, shift, 1) if shift else x


def split(x):
    high = x.astype(bf16)
    return high, (x - high.astype(f32)).astype(bf16)


def dot_nn(x, w):
    return lax.dot_general(x, w, (((1,), (0,)), ((), ())), preferred_element_type=f32)


def dot_nt(x, w):
    return lax.dot_general(x, w, (((1,), (1,)), ((), ())), preferred_element_type=f32)


def wide_times_exact(x, w, dot):
    n = x.shape[0]
    both = dot(jnp.concatenate(split(x), axis=0), w)
    return both[:n] + both[n:]


def stacked(x):
    high, low = split(x)
    return jnp.concatenate([high, low], axis=0), high


def times_parts(x, w):
    n = x[1].shape[0]
    both = dot_nn(x[0], w[0])
    out = both[:n] + both[n:]
    return out if w[1] is None else out + dot_nn(x[1], w[1])


def times(x, w):
    return times_parts(stacked(x), w)


def block_ids(shape):
    return (
        lax.broadcasted_iota(jnp.int32, shape, 0) // RANK,
        lax.broadcasted_iota(jnp.int32, shape, 1) // RANK,
    )


def placed(tiled, offset):
    tiled = jnp.concatenate([tiled, tiled], axis=1)
    row, col = block_ids(tiled.shape)
    return jnp.where(col == row + offset, tiled, 0.0)


def below(x, rows):
    return jnp.concatenate([x, jnp.zeros((rows - x.shape[0], x.shape[1]), x.dtype)], axis=0)


def above(x, rows):
    return jnp.concatenate([jnp.zeros((rows - x.shape[0], x.shape[1]), x.dtype), x], axis=0)


def in_two(tiled):
    return jnp.concatenate(split(tiled), axis=1)


def chained(x, w, count, shift, upward):
    rows = slice(0, WIDE - (count - 1) * RANK) if upward else slice((count - 1) * RANK, WIDE)
    moved = below(w[shift * RANK :], WIDE) if upward else above(w[: -shift * RANK], WIDE)
    out = dot_nn(jnp.concatenate(split(placed(x, 0)[rows]), axis=0), moved)
    n = out.shape[0] // 2
    out = out[:n] + out[n:]
    out = out[:, :128] + out[:, 128:]
    return below(out, WIDE) if upward else above(out, WIDE)


def leaving(parts, w):
    n = parts[1].shape[0]
    out = dot_nn(parts[0], w)
    out = out[:n] + out[n:]
    return out[:, :128] + out[:, 128:]


def carries(one, two, three, four, upward):
    sign = 1 if upward else -1
    row, col = block_ids((WIDE, WIDE))
    near = (
        lax.broadcasted_iota(jnp.int32, (WIDE, WIDE), 0)
        == lax.broadcasted_iota(jnp.int32, (WIDE, WIDE), 1)
    ).astype(f32)
    for step, x in ((1, one), (2, two), (3, three)):
        near = jnp.where(col == row + sign * step, jnp.concatenate([x, x], axis=1), near)
    half = slice(0, 128) if upward else slice(128, 256)
    row, col = block_ids((128, 128))
    far = in_two(jnp.where(col == row, four[half], 0.0))
    far = dot_nn(jnp.concatenate(split(near[half, half]), axis=1), jnp.concatenate([far, far], axis=0))
    far = far[:, :128] + far[:, 128:]
    low, high = near[:128], near[128:]
    if upward:
        low = jnp.concatenate([low[:, :128], low[:, 128:] + far], axis=1)
    else:
        high = jnp.concatenate([high[:, :128] + far, high[:, 128:]], axis=1)
    return jnp.concatenate([low, high], axis=0)


def joining(get, outward, exact):
    as_parts = (lambda w: (w.astype(bf16), None)) if exact else split
    t, r = get("T"), get("R")
    single = ((t, True), (r, False))
    tall = [in_two(x) for x, _ in single]
    twos = [chained(x, w, 2, 1, upward) for (x, upward), w in zip(single, tall)]
    yield
    tall = [in_two(x) for x in twos]
    fours = [chained(x, w, 4, 2, upward) for x, w, (_, upward) in zip(twos, tall, single)]
    threes = [chained(x, w, 3, 1, upward) for (x, upward), w in zip(single, tall)]
    yield
    up, down = (
        carries(*found, upward) for *found, (_, upward) in zip((t, r), twos, threes, fours, single)
    )
    yield
    gap = jnp.zeros((RANK, WIDE), f32)
    up_next = split(jnp.concatenate([up[RANK:], gap], axis=0))
    down_next = split(jnp.concatenate([gap, down[:-RANK]], axis=0))

    def with_rows(x, rows):
        return below(x, rows) if outward and x.shape[0] < rows else x

    e1 = times(get("o1"), up_next)
    d21 = as_parts(placed(get("A21"), 0))
    yield
    if outward:
        e1 = jnp.concatenate([e1, up[:RANK]], axis=0)
        dt, dr = above(in_two(t[-RANK:]), WIDE), below(in_two(r[:RANK]), WIDE)
    e1_parts = stacked(e1)
    q2 = with_rows(get("o2"), RHS + RANK) + times_parts(e1_parts, d21)
    yield
    e2 = times(q2, down_next)
    yield
    g31 = times_parts(e1_parts, as_parts(placed(get("A31"), 0)))
    if outward:
        g1 = leaving(e1_parts, dt)
        e2 = jnp.concatenate([e2, down[-RANK:]], axis=0)
    e2_parts = stacked(e2)
    g32 = times_parts(e2_parts, as_parts(placed(get("A32"), 0)))
    yield
    q3 = with_rows(get("o3"), ROWS) + with_rows(g31, ROWS) + g32
    e3 = times(q3, up_next)
    yield
    g41 = times_parts(e1_parts, as_parts(placed(get("A41"), 0)))
    g42 = times_parts(e2_parts, as_parts(placed(get("A42"), 0)))
    if outward:
        g2 = leaving(e2_parts, dr)
    e3_parts = stacked(e3)
    q4 = with_rows(get("o4"), ROWS) + with_rows(g41, ROWS) + g42 + times_parts(e3_parts, d21)
    yield
    e4 = times(q4, down_next)
    entering = (e1, e2, e3, e4)
    if not outward:
        return entering, None
    g3 = leaving(e3_parts, dt)
    g4 = leaving(stacked(e4), dr)
    last, first = slice(128, 256), slice(0, 128)
    group = lax.broadcasted_iota(jnp.int32, (ROWS, 128), 1) // RANK
    t1 = roll(with_rows(get("o1"), ROWS)[:, last], 32) + with_rows(g1, ROWS)
    t2 = roll(with_rows(q2, ROWS)[:, first], 32) + g2
    t3 = roll(q3[:, last], 96) + g3
    t4 = roll(q4[:, first], 96) + g4
    packed = jnp.where(
        group == 0, t1, jnp.where(group == 1, t2, jnp.where(group == 2, t3, t4))
    )
    return entering, packed


def joined(parts, outward, exact, between=iter(()), every=0):
    steps = joining(parts, outward, exact)
    while True:
        try:
            next(steps)
        except StopIteration as end:
            return end.value
        for _ in range(every):
            next(between, None)


def to_wire(packed):
    high, low = split(packed)
    low = low.astype(f32)
    half, group = RANK // 2, lax.broadcasted_iota(jnp.int32, (RANK // 2, 128), 1) // RANK
    t1, t2 = low[RHS : RHS + half], roll(low[RHS + half : RHS + RANK], 32)
    r1, r2 = roll(low[RHS + RANK : ROWS - half], 32), roll(low[ROWS - half :], 64)
    fine = jnp.where(group == 0, t1, jnp.where(group == 1, t2, jnp.where(group == 2, r1, r2)))
    return jnp.concatenate([high, fine.astype(bf16)], axis=0)


def unpack(received):
    received = received.astype(f32)
    received, fine = received[:, :ROWS], received[:, ROWS:]
    own = received[:, RHS : RHS + RANK].reshape(WIDE, 128)
    cross = received[:, RHS + RANK :].reshape(WIDE, 128)
    lane_group = lax.broadcasted_iota(jnp.int32, (WIDE, 128), 1) // RANK

    def tiled(x, group):
        x = jnp.where(lane_group[: x.shape[0]] == group, x, 0.0)
        x = x + roll(x, 32)
        return x + roll(x, 64)

    half = RANK // 2
    low = [tiled(fine.reshape(FAN * half, 128), g).reshape(FAN, half, 128) for g in range(4)]
    t = tiled(own, 0) + jnp.concatenate(low[:2], axis=1).reshape(WIDE, 128)
    r = tiled(cross, 1) + jnp.concatenate(low[2:], axis=1).reshape(WIDE, 128)
    maps = (
        t,
        r,
        tiled(own, 1),
        tiled(own, 2),
        tiled(cross, 2),
        tiled(own, 3),
        tiled(cross, 3),
    )
    group = lax.broadcasted_iota(jnp.int32, (RHS, 128), 1) // RANK
    offsets = []
    for k in range(4):
        halves = []
        for half in range(2):
            out = jnp.zeros((RHS, 128), f32)
            for g in range(4):
                moved = roll(received[4 * half + g, :RHS], 32 * (g - k))
                out = jnp.where(group == g, moved, out)
            halves.append(out)
        offsets.append(jnp.concatenate(halves, axis=1))
    found = dict(zip(("o1", "o2", "o3", "o4"), offsets))
    found.update(zip(("T", "R", "A21", "A31", "A32", "A41", "A42"), maps))
    return found.get


def own_piece(entering, piece):
    rows = entering[-1].shape[0]
    col = lax.broadcasted_iota(jnp.int32, (rows, WIDE), 1) // RANK
    group = lax.broadcasted_iota(jnp.int32, (rows, 128), 1) // RANK
    out = jnp.zeros((rows, 128), f32)
    for k, e in enumerate(entering):
        if e.shape[0] < rows:
            e = jnp.concatenate([e, jnp.zeros((rows - e.shape[0], WIDE), f32)], axis=0)
        e = jnp.where(col == piece, e, 0.0)
        e = e[:, :128] + e[:, 128:]
        e = e + roll(e, 32)
        e = e + roll(e, 64)
        out = jnp.where(group == k, e, out)
    return out


def place():
    index = lax.axis_index("rows")
    return lax.rem(index, FAN) // 2, lax.rem(index, 2), index // FAN


def moved_on(x):
    return jnp.where(lax.broadcasted_iota(jnp.int32, x.shape, 1) >= 64, roll(x, 64), 0.0)


def pieces_kernel(
    ranks_any, v_any, li_any, ll_any, lr_any, ui_any, ul_any, ur_any,
    wire_out, entering_out, rows_out, data_out,
    ranks, v, li, ll, lr, ui, ul, ur, sems,
):
    copies = {}

    def start(name, source, target, at):
        copies[name] = pltpu.make_async_copy(source, target, sems.at[at])
        copies[name].start()

    start("v", v_any, v, 0)
    start("ll", ll_any, ll, 1)
    start("a", li_any, li, 6)
    start("ul", ul_any, ul, 2)
    start("b", ui_any, ui, 7)
    start("lr", lr_any, lr, 3)
    start("ur", ur_any, ur, 4)
    start("ranks", ranks_any, ranks, 5)

    group = lax.broadcasted_iota(jnp.int32, (RHS, 128), 1) // RANK
    eye = (
        lax.broadcasted_iota(jnp.int32, (RANK, 128), 0)
        == lax.broadcasted_iota(jnp.int32, (RANK, 128), 1) % RANK
    ).astype(f32)
    blocks = range(FAN)
    span = [slice(BS * i, BS * (i + 1)) for i in blocks]
    k = RHS + RANK
    va, c, d, m, n, vab, cb, last = ([None] * FAN for _ in range(8))
    kept = {name: [] for name in ("T", "R", "A21", "A31", "A32", "A41", "A42", "o1", "o2", "o3", "o4")}

    def masked(right, rank):
        keep = lax.broadcasted_iota(jnp.int32, (RANK, BS), 0) < rank
        w = jnp.where(keep, right.astype(f32), 0.0).astype(bf16)
        return jnp.concatenate([w] * 4, axis=0)

    for name in ("v", "ll", "a"):
        copies[name].wait()
    for i in blocks:
        one = dot_nt(jnp.concatenate([v[:, span[i]], ll[i]], axis=0), li[i])
        va[i] = one[:RHS]
        c[i] = (-one[RHS:]).astype(bf16)
    for name in ("ul", "b", "lr", "ur", "ranks"):
        copies[name].wait()

    def work():
        for i in blocks:
            two = dot_nt(jnp.concatenate([*split(va[i]), c[i], ul[i]], axis=0), ui[i])
            vab[i] = two[:RHS] + two[RHS : 2 * RHS]
            cb[i] = two[2 * RHS : 2 * RHS + RANK]
            d[i] = (-two[2 * RHS + RANK :]).astype(bf16)
            yield
            m[i], n[i] = masked(lr[i], ranks[0, i]), masked(ur[i], ranks[1, i])
            w = dot_nt(jnp.concatenate([c[i], *split(va[i])], axis=0), m[i])
            kept["T"].append(eye + w[:RANK])
            kept["o1"].append(w[RANK:k] + w[k:])
            yield
        for i in blocks:
            both = split(jnp.concatenate([vab[i], cb[i]], axis=0))
            three = dot_nt(jnp.concatenate([*both, d[i]], axis=0), li[i])
            last[i] = jnp.concatenate([three[:k] + three[k : 2 * k], three[2 * k :]], axis=0)
            yield
            w = dot_nt(jnp.concatenate([d[i], *split(jnp.concatenate([vab[i], cb[i]], axis=0))], axis=0), n[i])
            kept["R"].append(eye + w[:RANK])
            w = w[RANK : RANK + k] + w[RANK + k :]
            kept["o2"].append(w[:RHS])
            kept["A21"].append(w[RHS:])
            yield
        four = [None] * FAN
        for i in blocks:
            four[i] = wide_times_exact(last[i], ui[i], dot_nt)
            rows_out[:, span[i]] = jnp.concatenate([four[i][RHS:], cb[i], d[i].astype(f32)], axis=0)
            data_out[:, span[i]] = jnp.concatenate([vab[i], four[i][:RHS]], axis=0)
            yield
            w = wide_times_exact(last[i], m[i], dot_nt)
            kept["o3"].append(w[:RHS])
            kept["A31"].append(w[RHS:k])
            kept["A32"].append(w[k:])
            yield
        for i in blocks:
            w = wide_times_exact(four[i], n[i], dot_nt)
            kept["o4"].append(w[:RHS])
            kept["A41"].append(w[RHS:k])
            kept["A42"].append(w[k:])
            yield

    between = work()

    def get(name):
        while len(kept[name]) < FAN:
            next(between)
        if name[0] != "o":
            return jnp.concatenate(kept[name], axis=0)
        halves = []
        for half in (kept[name][:4], kept[name][4:]):
            out = half[0]
            for g in range(1, 4):
                out = jnp.where(group == g, half[g], out)
            halves.append(out)
        return jnp.concatenate(halves, axis=1)

    entering, packed = joined(get, True, False, between, 4)
    wire_out[...] = to_wire(packed)
    for j, e in enumerate(entering):
        entering_out[j, : e.shape[0]] = e
        if e.shape[0] < ROWS:
            entering_out[j, e.shape[0] :] = jnp.zeros((ROWS - e.shape[0], WIDE), f32)


def response_kernel(entering, rows, data, high_out, low_out, base_out):
    entering = [entering[j] for j in range(4)]
    for i in range(FAN):
        span = slice(BS * i, BS * (i + 1))
        s = own_piece(entering, i)
        both = jnp.concatenate([s, moved_on(s)], axis=0)
        y = times(both, split(rows[:, span]))
        base_out[:, span] = data[:, span] + jnp.concatenate(
            [y[ROWS : ROWS + RHS], y[:RHS]], axis=0
        )
        gain = split(jnp.concatenate([y[RHS:ROWS], y[ROWS + RHS :]], axis=0))
        high_out[:, span] = gain[0]
        low_out[:, span] = gain[1]


def device_gain(own):
    s1, s2 = own[RHS : RHS + RANK], own[RHS + RANK :]
    return jnp.concatenate([s1, s2, moved_on(s1), moved_on(s2)], axis=0)


def plane_kernel(*refs):
    *pairs, wire_out, entering_out, received = refs
    chip, core, _ = place()
    for far, pair in enumerate(pairs):
        at = 2 * lax.rem(chip + 4 - far, 4)
        received[at + core] = pair[0]
        received[at + 1 - core] = pair[1]
    entering, packed = joined(unpack(received[...]), True, True)
    wire = to_wire(packed)
    for e in range(FAN):
        wire_out[e] = wire
    for k, e in enumerate(entering):
        entering_out[k, : e.shape[0]] = e
        if e.shape[0] < ROWS:
            entering_out[k, e.shape[0] :] = jnp.zeros((ROWS - e.shape[0], WIDE), f32)


def outputs_kernel(received, own, high, low, base, first_out, second_out):
    chip, core, at = place()
    own = own_piece([own[k] for k in range(4)], 2 * chip + core)
    gain = split(device_gain(own))
    entering, _ = joined(unpack(received[...]), False, True)
    plane = own_piece(entering, at)
    state = own[:RHS] + times(plane, gain)
    both = jnp.concatenate([moved_on(state), state], axis=0)
    y = base[...] + times(both, (high[...], low[...]))
    first_out[...] = y[:RHS]
    second_out[...] = y[RHS:]


vmem = pl.BlockSpec(memory_space=pltpu.VMEM)
hbm = pl.BlockSpec(memory_space=pltpu.HBM)


def call(kernel, name, out, specs, args, scratch=(), mib=16):
    return pl.pallas_call(
        kernel,
        out_shape=out,
        in_specs=specs,
        out_specs=jax.tree.map(lambda _: vmem, out),
        scratch_shapes=scratch,
        compiler_params=pltpu.CompilerParams(vmem_limit_bytes=mib << 20),
        name=name,
    )(*args)


def shape(*dims, dtype=f32):
    return jax.ShapeDtypeStruct(dims, dtype)


def local(
    right_sides, lower_inverse, lower_left, lower_right, upper_inverse, upper_left, upper_right, block_ranks
):
    order = right_sides.shape[1]
    n = lax.axis_size("rows")
    across = [[p * FAN + d for p in range(n // FAN)] for d in range(FAN)]
    to_core = [(i, i ^ 1) for i in range(n)]

    def along_y(far):
        return [(i, i // FAN * FAN + (i + 2 * far) % FAN) for i in range(n)]

    turned = [
        jnp.swapaxes(w, 1, 2) for w in (lower_left, lower_right, upper_left, upper_right)
    ]
    thin = pltpu.VMEM((FAN, RANK, BS), bf16)
    square = pltpu.VMEM((FAN, BS, BS), bf16)
    wire, entering, rows, data = call(
        pieces_kernel,
        "pieces",
        (
            shape(WIRE, 128, dtype=bf16),
            shape(4, ROWS, WIDE),
            shape(4 * RANK, order),
            shape(2 * RHS, order),
        ),
        [hbm] * 8,
        [
            pltpu.with_memory_space_constraint(x, pltpu.HBM)
            for x in (
                block_ranks, right_sides, lower_inverse, *turned[:2], upper_inverse, *turned[2:]
            )
        ],
        [
            pltpu.SMEM(block_ranks.shape, jnp.int32), pltpu.VMEM((RHS, order), bf16), square, thin, thin, square, thin, thin,
            pltpu.SemaphoreType.DMA((8,)),
        ],
    )
    pair = jnp.stack([wire, lax.ppermute(wire, "rows", to_core)])
    chips = [pair] + [lax.ppermute(pair, "rows", along_y(far)) for far in (1, 2, 3)]
    high, low, base = call(
        response_kernel,
        "response",
        (shape(4 * RANK, order, dtype=bf16), shape(4 * RANK, order, dtype=bf16), shape(2 * RHS, order)),
        [vmem] * 3,
        (entering, rows, data),
    )
    chips[2], high, low, base = lax.optimization_barrier((chips[2], high, low, base))
    wire, own = call(
        plane_kernel,
        "plane",
        (shape(FAN, WIRE, 128, dtype=bf16), shape(4, ROWS, WIDE)),
        [vmem] * 4,
        chips,
        [pltpu.VMEM((FAN, WIRE, 128), bf16)],
    )
    received = lax.all_to_all(wire, "rows", 0, 0, tiled=True, axis_index_groups=across)
    return call(
        outputs_kernel,
        "outputs",
        (shape(RHS, order), shape(RHS, order)),
        [vmem] * 5,
        (received, own, high, low, base),
    )


def solution(mesh):
    placed_in = (
        P("rhs", "rows"),
        P("rows", None, None),
        P("rows", None, None),
        P("rows", None, None),
        P("rows", None, None),
        P("rows", None, None),
        P("rows", None, None),
        P(None, "rows"),
    )
    return jax.shard_map(
        local,
        mesh=mesh,
        in_specs=placed_in,
        out_specs=(P("rhs", "rows"), P("rhs", "rows")),
        check_vma=False,
    )
```

```python
import functools

import jax
import jax.numpy as jnp
from jax import lax
from jax.experimental import pallas as pl
from jax.experimental.pallas import tpu as pltpu
from jax.sharding import PartitionSpec as P

f32, bf16 = jnp.float32, jnp.bfloat16

BS = 256
RANK = 32
RHS = 16
FAN = 8
WIDE = FAN * RANK
ROWS = RHS + 2 * RANK
WIRE = ROWS + RANK // 2


def roll(x, shift):
    shift %= x.shape[1]
    return pltpu.roll(x, shift, 1) if shift else x


def split(x):
    high = x.astype(bf16)
    return high, (x - high.astype(f32)).astype(bf16)


def dot_nn(x, w):
    return lax.dot_general(x, w, (((1,), (0,)), ((), ())), preferred_element_type=f32)


def dot_nt(x, w):
    return lax.dot_general(x, w, (((1,), (1,)), ((), ())), preferred_element_type=f32)


def wide_times_exact(x, w, dot):
    n = x.shape[0]
    both = dot(jnp.concatenate(split(x), axis=0), w)
    return both[:n] + both[n:]


def stacked(x):
    high, low = split(x)
    return jnp.concatenate([high, low], axis=0), high


def times_parts(x, w):
    n = x[1].shape[0]
    both = dot_nn(x[0], w[0])
    out = both[:n] + both[n:]
    return out if w[1] is None else out + dot_nn(x[1], w[1])


def times(x, w):
    return times_parts(stacked(x), w)


def block_ids(shape):
    return (
        lax.broadcasted_iota(jnp.int32, shape, 0) // RANK,
        lax.broadcasted_iota(jnp.int32, shape, 1) // RANK,
    )


def placed(tiled, offset):
    tiled = jnp.concatenate([tiled, tiled], axis=1)
    row, col = block_ids(tiled.shape)
    return jnp.where(col == row + offset, tiled, 0.0)


def below(x, rows):
    return jnp.concatenate([x, jnp.zeros((rows - x.shape[0], x.shape[1]), x.dtype)], axis=0)


def above(x, rows):
    return jnp.concatenate([jnp.zeros((rows - x.shape[0], x.shape[1]), x.dtype), x], axis=0)


def in_two(tiled):
    return jnp.concatenate(split(tiled), axis=1)


def chained(x, w, count, shift, upward):
    rows = slice(0, WIDE - (count - 1) * RANK) if upward else slice((count - 1) * RANK, WIDE)
    moved = below(w[shift * RANK :], WIDE) if upward else above(w[: -shift * RANK], WIDE)
    out = dot_nn(jnp.concatenate(split(placed(x, 0)[rows]), axis=0), moved)
    n = out.shape[0] // 2
    out = out[:n] + out[n:]
    out = out[:, :128] + out[:, 128:]
    return below(out, WIDE) if upward else above(out, WIDE)


def leaving(parts, w):
    n = parts[1].shape[0]
    out = dot_nn(parts[0], w)
    out = out[:n] + out[n:]
    return out[:, :128] + out[:, 128:]


def carries(one, two, three, four, upward):
    sign = 1 if upward else -1
    row, col = block_ids((WIDE, WIDE))
    near = (
        lax.broadcasted_iota(jnp.int32, (WIDE, WIDE), 0)
        == lax.broadcasted_iota(jnp.int32, (WIDE, WIDE), 1)
    ).astype(f32)
    for step, x in ((1, one), (2, two), (3, three)):
        near = jnp.where(col == row + sign * step, jnp.concatenate([x, x], axis=1), near)
    half = slice(0, 128) if upward else slice(128, 256)
    row, col = block_ids((128, 128))
    far = in_two(jnp.where(col == row, four[half], 0.0))
    far = dot_nn(jnp.concatenate(split(near[half, half]), axis=1), jnp.concatenate([far, far], axis=0))
    far = far[:, :128] + far[:, 128:]
    low, high = near[:128], near[128:]
    if upward:
        low = jnp.concatenate([low[:, :128], low[:, 128:] + far], axis=1)
    else:
        high = jnp.concatenate([high[:, :128] + far, high[:, 128:]], axis=1)
    return jnp.concatenate([low, high], axis=0)


def joining(get, outward, exact):
    as_parts = (lambda w: (w.astype(bf16), None)) if exact else split
    t, r = get("T"), get("R")
    single = ((t, True), (r, False))
    tall = [in_two(x) for x, _ in single]
    twos = [chained(x, w, 2, 1, upward) for (x, upward), w in zip(single, tall)]
    yield
    tall = [in_two(x) for x in twos]
    fours = [chained(x, w, 4, 2, upward) for x, w, (_, upward) in zip(twos, tall, single)]
    threes = [chained(x, w, 3, 1, upward) for (x, upward), w in zip(single, tall)]
    yield
    up, down = (
        carries(*found, upward) for *found, (_, upward) in zip((t, r), twos, threes, fours, single)
    )
    yield
    gap = jnp.zeros((RANK, WIDE), f32)
    up_next = split(jnp.concatenate([up[RANK:], gap], axis=0))
    down_next = split(jnp.concatenate([gap, down[:-RANK]], axis=0))

    def with_rows(x, rows):
        return below(x, rows) if outward and x.shape[0] < rows else x

    e1 = times(get("o1"), up_next)
    d21 = as_parts(placed(get("A21"), 0))
    yield
    if outward:
        e1 = jnp.concatenate([e1, up[:RANK]], axis=0)
        dt, dr = above(in_two(t[-RANK:]), WIDE), below(in_two(r[:RANK]), WIDE)
    e1_parts = stacked(e1)
    q2 = with_rows(get("o2"), RHS + RANK) + times_parts(e1_parts, d21)
    yield
    e2 = times(q2, down_next)
    yield
    g31 = times_parts(e1_parts, as_parts(placed(get("A31"), 0)))
    if outward:
        g1 = leaving(e1_parts, dt)
        e2 = jnp.concatenate([e2, down[-RANK:]], axis=0)
    e2_parts = stacked(e2)
    g32 = times_parts(e2_parts, as_parts(placed(get("A32"), 0)))
    yield
    q3 = with_rows(get("o3"), ROWS) + with_rows(g31, ROWS) + g32
    e3 = times(q3, up_next)
    yield
    g41 = times_parts(e1_parts, as_parts(placed(get("A41"), 0)))
    g42 = times_parts(e2_parts, as_parts(placed(get("A42"), 0)))
    if outward:
        g2 = leaving(e2_parts, dr)
    e3_parts = stacked(e3)
    q4 = with_rows(get("o4"), ROWS) + with_rows(g41, ROWS) + g42 + times_parts(e3_parts, d21)
    yield
    e4 = times(q4, down_next)
    entering = (e1, e2, e3, e4)
    if not outward:
        return entering, None
    g3 = leaving(e3_parts, dt)
    g4 = leaving(stacked(e4), dr)
    last, first = slice(128, 256), slice(0, 128)
    group = lax.broadcasted_iota(jnp.int32, (ROWS, 128), 1) // RANK
    t1 = roll(with_rows(get("o1"), ROWS)[:, last], 32) + with_rows(g1, ROWS)
    t2 = roll(with_rows(q2, ROWS)[:, first], 32) + g2
    t3 = roll(q3[:, last], 96) + g3
    t4 = roll(q4[:, first], 96) + g4
    packed = jnp.where(
        group == 0, t1, jnp.where(group == 1, t2, jnp.where(group == 2, t3, t4))
    )
    return entering, packed


def joined(parts, outward, exact, between=iter(()), every=0):
    steps = joining(parts, outward, exact)
    while True:
        try:
            next(steps)
        except StopIteration as end:
            return end.value
        for _ in range(every):
            next(between, None)


def to_wire(packed):
    high, low = split(packed)
    low = low.astype(f32)
    half, group = RANK // 2, lax.broadcasted_iota(jnp.int32, (RANK // 2, 128), 1) // RANK
    t1, t2 = low[RHS : RHS + half], roll(low[RHS + half : RHS + RANK], 32)
    r1, r2 = roll(low[RHS + RANK : ROWS - half], 32), roll(low[ROWS - half :], 64)
    fine = jnp.where(group == 0, t1, jnp.where(group == 1, t2, jnp.where(group == 2, r1, r2)))
    return jnp.concatenate([high, fine.astype(bf16)], axis=0)


def unpack(received):
    received, fine = received[:, :ROWS], received[:, ROWS:]
    own = received[:, RHS : RHS + RANK].reshape(WIDE, 128)
    cross = received[:, RHS + RANK :].reshape(WIDE, 128)
    lane_group = lax.broadcasted_iota(jnp.int32, (WIDE, 128), 1) // RANK

    def tiled(x, group):
        x = jnp.where(lane_group[: x.shape[0]] == group, x, jnp.zeros_like(x))
        x = x + roll(x, 32)
        return (x + roll(x, 64)).astype(f32)

    half = RANK // 2
    low = [tiled(fine.reshape(FAN * half, 128), g).reshape(FAN, half, 128) for g in range(4)]
    t = tiled(own, 0) + jnp.concatenate(low[:2], axis=1).reshape(WIDE, 128)
    r = tiled(cross, 1) + jnp.concatenate(low[2:], axis=1).reshape(WIDE, 128)
    maps = (
        t,
        r,
        tiled(own, 1),
        tiled(own, 2),
        tiled(cross, 2),
        tiled(own, 3),
        tiled(cross, 3),
    )
    group = lax.broadcasted_iota(jnp.int32, (RHS, 128), 1) // RANK
    offsets = []
    for k in range(4):
        halves = []
        for half in range(2):
            out = jnp.zeros((RHS, 128), f32)
            for g in range(4):
                moved = roll(received[4 * half + g, :RHS].astype(f32), 32 * (g - k))
                out = jnp.where(group == g, moved, out)
            halves.append(out)
        offsets.append(jnp.concatenate(halves, axis=1))
    found = dict(zip(("o1", "o2", "o3", "o4"), offsets))
    found.update(zip(("T", "R", "A21", "A31", "A32", "A41", "A42"), maps))
    return found.get


def own_piece(entering, piece):
    rows = entering[-1].shape[0]
    col = lax.broadcasted_iota(jnp.int32, (rows, WIDE), 1) // RANK
    group = lax.broadcasted_iota(jnp.int32, (rows, 128), 1) // RANK
    out = jnp.zeros((rows, 128), f32)
    for k, e in enumerate(entering):
        if e.shape[0] < rows:
            e = jnp.concatenate([e, jnp.zeros((rows - e.shape[0], WIDE), f32)], axis=0)
        e = jnp.where(col == piece, e, 0.0)
        e = e[:, :128] + e[:, 128:]
        e = e + roll(e, 32)
        e = e + roll(e, 64)
        out = jnp.where(group == k, e, out)
    return out


def place():
    index = lax.axis_index("rows")
    return lax.rem(index, FAN) // 2, lax.rem(index, 2), index // FAN


def moved_on(x):
    return jnp.where(lax.broadcasted_iota(jnp.int32, x.shape, 1) >= 64, roll(x, 64), 0.0)


def pieces_kernel(
    ranks_any, v_any, li_any, ll_any, lr_any, ui_any, ul_any, ur_any,
    wire_out, entering_out, rows_out, data_out,
    ranks, v, li, ll, lr, ui, ul, ur, sems,
):
    copies = {}

    def start(name, source, target, at):
        copies[name] = pltpu.make_async_copy(source, target, sems.at[at])
        copies[name].start()

    start("v", v_any, v, 0)
    start("ll", ll_any, ll, 1)
    start("a", li_any, li, 6)
    start("ul", ul_any, ul, 2)
    start("b", ui_any, ui, 7)
    start("lr", lr_any, lr, 3)
    start("ur", ur_any, ur, 4)
    start("ranks", ranks_any, ranks, 5)

    group = lax.broadcasted_iota(jnp.int32, (RHS, 128), 1) // RANK
    eye = (
        lax.broadcasted_iota(jnp.int32, (RANK, 128), 0)
        == lax.broadcasted_iota(jnp.int32, (RANK, 128), 1) % RANK
    ).astype(f32)
    blocks = range(FAN)
    span = [slice(BS * i, BS * (i + 1)) for i in blocks]
    k = RHS + RANK
    va, c, d, m, n, vab, cb, last = ([None] * FAN for _ in range(8))
    kept = {name: [] for name in ("T", "R", "A21", "A31", "A32", "A41", "A42", "o1", "o2", "o3", "o4")}

    def masked(right, rank):
        keep = lax.broadcasted_iota(jnp.int32, (RANK, BS), 0) < rank
        w = jnp.where(keep, right.astype(f32), 0.0).astype(bf16)
        return jnp.concatenate([w] * 4, axis=0)

    for name in ("v", "ll", "a"):
        copies[name].wait()
    for i in blocks:
        one = dot_nt(jnp.concatenate([v[:, span[i]], ll[i]], axis=0), li[i])
        va[i] = one[:RHS]
        c[i] = (-one[RHS:]).astype(bf16)
    for name in ("ul", "b", "lr", "ur", "ranks"):
        copies[name].wait()

    def work():
        for i in blocks:
            two = dot_nt(jnp.concatenate([*split(va[i]), c[i], ul[i]], axis=0), ui[i])
            vab[i] = two[:RHS] + two[RHS : 2 * RHS]
            cb[i] = two[2 * RHS : 2 * RHS + RANK]
            d[i] = (-two[2 * RHS + RANK :]).astype(bf16)
            yield
            m[i], n[i] = masked(lr[i], ranks[0, i]), masked(ur[i], ranks[1, i])
            w = dot_nt(jnp.concatenate([c[i], *split(va[i])], axis=0), m[i])
            kept["T"].append(eye + w[:RANK])
            kept["o1"].append(w[RANK:k] + w[k:])
            yield
        for i in blocks:
            both = split(jnp.concatenate([vab[i], cb[i]], axis=0))
            three = dot_nt(jnp.concatenate([*both, d[i]], axis=0), li[i])
            last[i] = jnp.concatenate([three[:k] + three[k : 2 * k], three[2 * k :]], axis=0)
            yield
            w = dot_nt(jnp.concatenate([d[i], *split(jnp.concatenate([vab[i], cb[i]], axis=0))], axis=0), n[i])
            kept["R"].append(eye + w[:RANK])
            w = w[RANK : RANK + k] + w[RANK + k :]
            kept["o2"].append(w[:RHS])
            kept["A21"].append(w[RHS:])
            yield
        four = [None] * FAN
        for i in blocks:
            four[i] = wide_times_exact(last[i], ui[i], dot_nt)
            rows_out[:, span[i]] = jnp.concatenate([four[i][RHS:], cb[i], d[i].astype(f32)], axis=0)
            data_out[:, span[i]] = jnp.concatenate([vab[i], four[i][:RHS]], axis=0)
            yield
            w = wide_times_exact(last[i], m[i], dot_nt)
            kept["o3"].append(w[:RHS])
            kept["A31"].append(w[RHS:k])
            kept["A32"].append(w[k:])
            yield
        for i in blocks:
            w = wide_times_exact(four[i], n[i], dot_nt)
            kept["o4"].append(w[:RHS])
            kept["A41"].append(w[RHS:k])
            kept["A42"].append(w[k:])
            yield

    between = work()

    def get(name):
        while len(kept[name]) < FAN:
            next(between)
        if name[0] != "o":
            return jnp.concatenate(kept[name], axis=0)
        halves = []
        for half in (kept[name][:4], kept[name][4:]):
            out = half[0]
            for g in range(1, 4):
                out = jnp.where(group == g, half[g], out)
            halves.append(out)
        return jnp.concatenate(halves, axis=1)

    entering, packed = joined(get, True, True, between, 4)
    wire_out[...] = to_wire(packed)
    for j, e in enumerate(entering):
        entering_out[j, : e.shape[0]] = e
        if e.shape[0] < ROWS:
            entering_out[j, e.shape[0] :] = jnp.zeros((ROWS - e.shape[0], WIDE), f32)


def response_kernel(entering, rows, data, high_out, low_out, base_out):
    entering = [entering[j] for j in range(4)]
    for i in range(FAN):
        span = slice(BS * i, BS * (i + 1))
        s = own_piece(entering, i)
        both = jnp.concatenate([s, moved_on(s)], axis=0)
        y = times(both, split(rows[:, span]))
        base_out[:, span] = data[:, span] + jnp.concatenate(
            [y[ROWS : ROWS + RHS], y[:RHS]], axis=0
        )
        gain = split(jnp.concatenate([y[RHS:ROWS], y[ROWS + RHS :]], axis=0))
        high_out[:, span] = gain[0]
        low_out[:, span] = gain[1]


def device_gain(own):
    s1, s2 = own[RHS : RHS + RANK], own[RHS + RANK :]
    return jnp.concatenate([s1, s2, moved_on(s1), moved_on(s2)], axis=0)


def plane_kernel(*refs):
    *pairs, wire_out, entering_out, received = refs
    chip, core, _ = place()
    for far, pair in enumerate(pairs):
        at = 2 * lax.rem(chip + 4 - far, 4)
        received[at + core] = pair[0]
        received[at + 1 - core] = pair[1]
    entering, packed = joined(unpack(received[...]), True, True)
    wire = to_wire(packed)
    for e in range(FAN):
        wire_out[e] = wire
    for k, e in enumerate(entering):
        entering_out[k, : e.shape[0]] = e
        if e.shape[0] < ROWS:
            entering_out[k, e.shape[0] :] = jnp.zeros((ROWS - e.shape[0], WIDE), f32)


def outputs_kernel(received, own, high, low, base, first_out, second_out):
    chip, core, at = place()
    own = own_piece([own[k] for k in range(4)], 2 * chip + core)
    gain = split(device_gain(own))
    entering, _ = joined(unpack(received[...]), False, True)
    plane = own_piece(entering, at)
    state = own[:RHS] + times(plane, gain)
    both = jnp.concatenate([moved_on(state), state], axis=0)
    y = base[...] + times(both, (high[...], low[...]))
    first_out[...] = y[:RHS]
    second_out[...] = y[RHS:]


vmem = pl.BlockSpec(memory_space=pltpu.VMEM)
hbm = pl.BlockSpec(memory_space=pltpu.HBM)


def call(kernel, name, out, specs, args, scratch=(), mib=16):
    return pl.pallas_call(
        kernel,
        out_shape=out,
        in_specs=specs,
        out_specs=jax.tree.map(lambda _: vmem, out),
        scratch_shapes=scratch,
        compiler_params=pltpu.CompilerParams(vmem_limit_bytes=mib << 20),
        name=name,
    )(*args)


def shape(*dims, dtype=f32):
    return jax.ShapeDtypeStruct(dims, dtype)


def local(
    right_sides, lower_inverse, lower_left, lower_right, upper_inverse, upper_left, upper_right, block_ranks
):
    order = right_sides.shape[1]
    n = lax.axis_size("rows")
    across = [[p * FAN + d for p in range(n // FAN)] for d in range(FAN)]
    to_core = [(i, i ^ 1) for i in range(n)]

    def along_y(far):
        return [(i, i // FAN * FAN + (i + 2 * far) % FAN) for i in range(n)]

    turned = [
        jnp.swapaxes(w, 1, 2) for w in (lower_left, lower_right, upper_left, upper_right)
    ]
    thin = pltpu.VMEM((FAN, RANK, BS), bf16)
    square = pltpu.VMEM((FAN, BS, BS), bf16)
    wire, entering, rows, data = call(
        pieces_kernel,
        "pieces",
        (
            shape(WIRE, 128, dtype=bf16),
            shape(4, ROWS, WIDE),
            shape(4 * RANK, order),
            shape(2 * RHS, order),
        ),
        [hbm] * 8,
        [
            pltpu.with_memory_space_constraint(x, pltpu.HBM)
            for x in (
                block_ranks, right_sides, lower_inverse, *turned[:2], upper_inverse, *turned[2:]
            )
        ],
        [
            pltpu.SMEM(block_ranks.shape, jnp.int32), pltpu.VMEM((RHS, order), bf16), square, thin, thin, square, thin, thin,
            pltpu.SemaphoreType.DMA((8,)),
        ],
    )
    pair = jnp.stack([wire, lax.ppermute(wire, "rows", to_core)])
    chips = [pair] + [lax.ppermute(pair, "rows", along_y(far)) for far in (1, 2, 3)]
    high, low, base = call(
        response_kernel,
        "response",
        (shape(4 * RANK, order, dtype=bf16), shape(4 * RANK, order, dtype=bf16), shape(2 * RHS, order)),
        [vmem] * 3,
        (entering, rows, data),
    )
    chips[2], high, low, base = lax.optimization_barrier((chips[2], high, low, base))
    wire, own = call(
        plane_kernel,
        "plane",
        (shape(FAN, WIRE, 128, dtype=bf16), shape(4, ROWS, WIDE)),
        [vmem] * 4,
        chips,
        [pltpu.VMEM((FAN, WIRE, 128), bf16)],
    )
    received = lax.all_to_all(wire, "rows", 0, 0, tiled=True, axis_index_groups=across)
    return call(
        outputs_kernel,
        "outputs",
        (shape(RHS, order), shape(RHS, order)),
        [vmem] * 5,
        (received, own, high, low, base),
    )


def solution(mesh):
    placed_in = (
        P("rhs", "rows"),
        P("rows", None, None),
        P("rows", None, None),
        P("rows", None, None),
        P("rows", None, None),
        P("rows", None, None),
        P("rows", None, None),
        P(None, "rows"),
    )
    return jax.shard_map(
        local,
        mesh=mesh,
        in_specs=placed_in,
        out_specs=(P("rhs", "rows"), P("rhs", "rows")),
        check_vma=False,
    )
```

```python
import functools

import jax
import jax.numpy as jnp
from jax import lax
from jax.experimental import pallas as pl
from jax.experimental.pallas import tpu as pltpu
from jax.sharding import PartitionSpec as P

f32, bf16 = jnp.float32, jnp.bfloat16

BS = 256
RANK = 32
RHS = 16
FAN = 8
WIDE = FAN * RANK
ROWS = RHS + 2 * RANK
WIRE = ROWS + RANK // 2


def roll(x, shift):
    shift %= x.shape[1]
    return pltpu.roll(x, shift, 1) if shift else x


def split(x):
    high = x.astype(bf16)
    return high, (x - high.astype(f32)).astype(bf16)


def dot_nn(x, w):
    return lax.dot_general(x, w, (((1,), (0,)), ((), ())), preferred_element_type=f32)


def dot_nt(x, w):
    return lax.dot_general(x, w, (((1,), (1,)), ((), ())), preferred_element_type=f32)


def wide_times_exact(x, w, dot):
    n = x.shape[0]
    both = dot(jnp.concatenate(split(x), axis=0), w)
    return both[:n] + both[n:]


def stacked(x):
    high, low = split(x)
    return jnp.concatenate([high, low], axis=0), high


def times_parts(x, w):
    n = x[1].shape[0]
    both = dot_nn(x[0], w[0])
    out = both[:n] + both[n:]
    return out if w[1] is None else out + dot_nn(x[1], w[1])


def times(x, w):
    return times_parts(stacked(x), w)


def block_ids(shape):
    return (
        lax.broadcasted_iota(jnp.int32, shape, 0) // RANK,
        lax.broadcasted_iota(jnp.int32, shape, 1) // RANK,
    )


def placed(tiled, offset):
    tiled = jnp.concatenate([tiled, tiled], axis=1)
    row, col = block_ids(tiled.shape)
    return jnp.where(col == row + offset, tiled, 0.0)


def below(x, rows):
    return jnp.concatenate([x, jnp.zeros((rows - x.shape[0], x.shape[1]), x.dtype)], axis=0)


def above(x, rows):
    return jnp.concatenate([jnp.zeros((rows - x.shape[0], x.shape[1]), x.dtype), x], axis=0)


def in_two(tiled):
    return jnp.concatenate(split(tiled), axis=1)


def chained(x, w, count, shift, upward):
    rows = slice(0, WIDE - count * RANK) if upward else slice(count * RANK, WIDE)
    moved = below(w[shift * RANK :], WIDE) if upward else above(w[: -shift * RANK], WIDE)
    out = dot_nn(jnp.concatenate(split(placed(x, 0)[rows]), axis=0), moved)
    n = out.shape[0] // 2
    out = out[:n] + out[n:]
    out = out[:, :128] + out[:, 128:]
    return below(out, WIDE) if upward else above(out, WIDE)


def leaving(parts, w):
    n = parts[1].shape[0]
    out = dot_nn(parts[0], w)
    out = out[:n] + out[n:]
    return out[:, :128] + out[:, 128:]


def carries(one, two, three, four, upward):
    sign = 1 if upward else -1
    row, col = block_ids((WIDE, WIDE))
    near = (
        lax.broadcasted_iota(jnp.int32, (WIDE, WIDE), 0)
        == lax.broadcasted_iota(jnp.int32, (WIDE, WIDE), 1)
    ).astype(f32)
    for step, x in ((1, one), (2, two), (3, three)):
        near = jnp.where(col == row + sign * step, jnp.concatenate([x, x], axis=1), near)
    half = slice(0, 128) if upward else slice(128, 256)
    row, col = block_ids((128, 128))
    far = in_two(jnp.where(col == row, four[half], 0.0))
    far = dot_nn(jnp.concatenate(split(near[half, half]), axis=1), jnp.concatenate([far, far], axis=0))
    far = far[:, :128] + far[:, 128:]
    low, high = near[:128], near[128:]
    if upward:
        low = jnp.concatenate([low[:, :128], low[:, 128:] + far], axis=1)
    else:
        high = jnp.concatenate([high[:, :128] + far, high[:, 128:]], axis=1)
    return jnp.concatenate([low, high], axis=0)


def joining(get, outward, exact):
    as_parts = (lambda w: (w.astype(bf16), None)) if exact else split
    t, r = get("T"), get("R")
    single = ((t, True), (r, False))
    tall = [in_two(x) for x, _ in single]
    twos = [chained(x, w, 2, 1, upward) for (x, upward), w in zip(single, tall)]
    yield
    tall = [in_two(x) for x in twos]
    fours = [chained(x, w, 4, 2, upward) for x, w, (_, upward) in zip(twos, tall, single)]
    threes = [chained(x, w, 3, 1, upward) for (x, upward), w in zip(single, tall)]
    yield
    up, down = (
        carries(*found, upward) for *found, (_, upward) in zip((t, r), twos, threes, fours, single)
    )
    yield
    gap = jnp.zeros((RANK, WIDE), f32)
    up_next = split(jnp.concatenate([up[RANK:], gap], axis=0))
    down_next = split(jnp.concatenate([gap, down[:-RANK]], axis=0))

    def with_rows(x, rows):
        return below(x, rows) if outward and x.shape[0] < rows else x

    e1 = times(get("o1"), up_next)
    d21 = as_parts(placed(get("A21"), 0))
    yield
    if outward:
        e1 = jnp.concatenate([e1, up[:RANK]], axis=0)
        dt, dr = above(in_two(t[-RANK:]), WIDE), below(in_two(r[:RANK]), WIDE)
    e1_parts = stacked(e1)
    q2 = with_rows(get("o2"), RHS + RANK) + times_parts(e1_parts, d21)
    yield
    e2 = times(q2, down_next)
    yield
    g31 = times_parts(e1_parts, as_parts(placed(get("A31"), 0)))
    if outward:
        g1 = leaving(e1_parts, dt)
        e2 = jnp.concatenate([e2, down[-RANK:]], axis=0)
    e2_parts = stacked(e2)
    g32 = times_parts(e2_parts, as_parts(placed(get("A32"), 0)))
    yield
    q3 = with_rows(get("o3"), ROWS) + with_rows(g31, ROWS) + g32
    e3 = times(q3, up_next)
    yield
    g41 = times_parts(e1_parts, as_parts(placed(get("A41"), 0)))
    g42 = times_parts(e2_parts, as_parts(placed(get("A42"), 0)))
    if outward:
        g2 = leaving(e2_parts, dr)
    e3_parts = stacked(e3)
    q4 = with_rows(get("o4"), ROWS) + with_rows(g41, ROWS) + g42 + times_parts(e3_parts, d21)
    yield
    e4 = times(q4, down_next)
    entering = (e1, e2, e3, e4)
    if not outward:
        return entering, None
    g3 = leaving(e3_parts, dt)
    g4 = leaving(stacked(e4), dr)
    last, first = slice(128, 256), slice(0, 128)
    group = lax.broadcasted_iota(jnp.int32, (ROWS, 128), 1) // RANK
    t1 = roll(with_rows(get("o1"), ROWS)[:, last], 32) + with_rows(g1, ROWS)
    t2 = roll(with_rows(q2, ROWS)[:, first], 32) + g2
    t3 = roll(q3[:, last], 96) + g3
    t4 = roll(q4[:, first], 96) + g4
    packed = jnp.where(
        group == 0, t1, jnp.where(group == 1, t2, jnp.where(group == 2, t3, t4))
    )
    return entering, packed


def joined(parts, outward, exact, between=iter(()), every=0):
    steps = joining(parts, outward, exact)
    while True:
        try:
            next(steps)
        except StopIteration as end:
            return end.value
        for _ in range(every):
            next(between, None)


def to_wire(packed):
    high, low = split(packed)
    low = low.astype(f32)
    half, group = RANK // 2, lax.broadcasted_iota(jnp.int32, (RANK // 2, 128), 1) // RANK
    t1, t2 = low[RHS : RHS + half], roll(low[RHS + half : RHS + RANK], 32)
    r1, r2 = roll(low[RHS + RANK : ROWS - half], 32), roll(low[ROWS - half :], 64)
    fine = jnp.where(group == 0, t1, jnp.where(group == 1, t2, jnp.where(group == 2, r1, r2)))
    return jnp.concatenate([high, fine.astype(bf16)], axis=0)


def unpack(received):
    received, fine = received[:, :ROWS], received[:, ROWS:]
    own = received[:, RHS : RHS + RANK].reshape(WIDE, 128)
    cross = received[:, RHS + RANK :].reshape(WIDE, 128)
    lane_group = lax.broadcasted_iota(jnp.int32, (WIDE, 128), 1) // RANK

    def tiled(x, group):
        x = jnp.where(lane_group[: x.shape[0]] == group, x, jnp.zeros_like(x))
        x = x + roll(x, 32)
        return (x + roll(x, 64)).astype(f32)

    half = RANK // 2
    low = [tiled(fine.reshape(FAN * half, 128), g).reshape(FAN, half, 128) for g in range(4)]
    t = tiled(own, 0) + jnp.concatenate(low[:2], axis=1).reshape(WIDE, 128)
    r = tiled(cross, 1) + jnp.concatenate(low[2:], axis=1).reshape(WIDE, 128)
    maps = (
        t,
        r,
        tiled(own, 1),
        tiled(own, 2),
        tiled(cross, 2),
        tiled(own, 3),
        tiled(cross, 3),
    )
    group = lax.broadcasted_iota(jnp.int32, (RHS, 128), 1) // RANK
    offsets = []
    for k in range(4):
        halves = []
        for half in range(2):
            out = jnp.zeros((RHS, 128), f32)
            for g in range(4):
                moved = roll(received[4 * half + g, :RHS].astype(f32), 32 * (g - k))
                out = jnp.where(group == g, moved, out)
            halves.append(out)
        offsets.append(jnp.concatenate(halves, axis=1))
    found = dict(zip(("o1", "o2", "o3", "o4"), offsets))
    found.update(zip(("T", "R", "A21", "A31", "A32", "A41", "A42"), maps))
    return found.get


def own_piece(entering, piece):
    rows = entering[-1].shape[0]
    col = lax.broadcasted_iota(jnp.int32, (rows, WIDE), 1) // RANK
    group = lax.broadcasted_iota(jnp.int32, (rows, 128), 1) // RANK
    out = jnp.zeros((rows, 128), f32)
    for k, e in enumerate(entering):
        if e.shape[0] < rows:
            e = jnp.concatenate([e, jnp.zeros((rows - e.shape[0], WIDE), f32)], axis=0)
        e = jnp.where(col == piece, e, 0.0)
        e = e[:, :128] + e[:, 128:]
        e = e + roll(e, 32)
        e = e + roll(e, 64)
        out = jnp.where(group == k, e, out)
    return out


def place():
    index = lax.axis_index("rows")
    return lax.rem(index, FAN) // 2, lax.rem(index, 2), index // FAN


def moved_on(x):
    return jnp.where(lax.broadcasted_iota(jnp.int32, x.shape, 1) >= 64, roll(x, 64), 0.0)


def pieces_kernel(
    ranks_any, v_any, li_any, ll_any, lr_any, ui_any, ul_any, ur_any,
    wire_out, entering_out, rows_out, data_out,
    ranks, v, li, ll, lr, ui, ul, ur, sems,
):
    copies = {}

    def start(name, source, target, at):
        copies[name] = pltpu.make_async_copy(source, target, sems.at[at])
        copies[name].start()

    start("v", v_any, v, 0)
    start("ll", ll_any, ll, 1)
    start("a", li_any, li, 6)
    start("ul", ul_any, ul, 2)
    start("b", ui_any, ui, 7)
    start("lr", lr_any, lr, 3)
    start("ur", ur_any, ur, 4)
    start("ranks", ranks_any, ranks, 5)

    group = lax.broadcasted_iota(jnp.int32, (RHS, 128), 1) // RANK
    eye = (
        lax.broadcasted_iota(jnp.int32, (RANK, 128), 0)
        == lax.broadcasted_iota(jnp.int32, (RANK, 128), 1) % RANK
    ).astype(f32)
    blocks = range(FAN)
    span = [slice(BS * i, BS * (i + 1)) for i in blocks]
    k = RHS + RANK
    va, c, d, m, n, vab, cb, last = ([None] * FAN for _ in range(8))
    kept = {name: [] for name in ("T", "R", "A21", "A31", "A32", "A41", "A42", "o1", "o2", "o3", "o4")}

    def masked(right, rank):
        keep = lax.broadcasted_iota(jnp.int32, (RANK, BS), 0) < rank
        w = jnp.where(keep, right.astype(f32), 0.0).astype(bf16)
        return jnp.concatenate([w] * 4, axis=0)

    for name in ("v", "ll", "a"):
        copies[name].wait()
    for i in blocks:
        one = dot_nt(jnp.concatenate([v[:, span[i]], ll[i]], axis=0), li[i])
        va[i] = one[:RHS]
        c[i] = (-one[RHS:]).astype(bf16)
    for name in ("ul", "b", "lr", "ur", "ranks"):
        copies[name].wait()

    def work():
        for i in blocks:
            two = dot_nt(jnp.concatenate([*split(va[i]), c[i], ul[i]], axis=0), ui[i])
            vab[i] = two[:RHS] + two[RHS : 2 * RHS]
            cb[i] = two[2 * RHS : 2 * RHS + RANK]
            d[i] = (-two[2 * RHS + RANK :]).astype(bf16)
            yield
            m[i], n[i] = masked(lr[i], ranks[0, i]), masked(ur[i], ranks[1, i])
            w = dot_nt(jnp.concatenate([c[i], *split(va[i])], axis=0), m[i])
            kept["T"].append(eye + w[:RANK])
            kept["o1"].append(w[RANK:k] + w[k:])
            yield
        for i in blocks:
            both = split(jnp.concatenate([vab[i], cb[i]], axis=0))
            three = dot_nt(jnp.concatenate([*both, d[i]], axis=0), li[i])
            last[i] = jnp.concatenate([three[:k] + three[k : 2 * k], three[2 * k :]], axis=0)
            yield
            w = dot_nt(jnp.concatenate([d[i], *split(jnp.concatenate([vab[i], cb[i]], axis=0))], axis=0), n[i])
            kept["R"].append(eye + w[:RANK])
            w = w[RANK : RANK + k] + w[RANK + k :]
            kept["o2"].append(w[:RHS])
            kept["A21"].append(w[RHS:])
            yield
        four = [None] * FAN
        for i in blocks:
            four[i] = wide_times_exact(last[i], ui[i], dot_nt)
            rows_out[:, span[i]] = jnp.concatenate([four[i][RHS:], cb[i], d[i].astype(f32)], axis=0)
            data_out[:, span[i]] = jnp.concatenate([vab[i], four[i][:RHS]], axis=0)
            yield
            w = wide_times_exact(last[i], m[i], dot_nt)
            kept["o3"].append(w[:RHS])
            kept["A31"].append(w[RHS:k])
            kept["A32"].append(w[k:])
            yield
        for i in blocks:
            w = wide_times_exact(four[i], n[i], dot_nt)
            kept["o4"].append(w[:RHS])
            kept["A41"].append(w[RHS:k])
            kept["A42"].append(w[k:])
            yield

    between = work()

    def get(name):
        while len(kept[name]) < FAN:
            next(between)
        if name[0] != "o":
            return jnp.concatenate(kept[name], axis=0)
        halves = []
        for half in (kept[name][:4], kept[name][4:]):
            out = half[0]
            for g in range(1, 4):
                out = jnp.where(group == g, half[g], out)
            halves.append(out)
        return jnp.concatenate(halves, axis=1)

    entering, packed = joined(get, True, True, between, 4)
    wire_out[...] = to_wire(packed)
    for j, e in enumerate(entering):
        entering_out[j, : e.shape[0]] = e
        if e.shape[0] < ROWS:
            entering_out[j, e.shape[0] :] = jnp.zeros((ROWS - e.shape[0], WIDE), f32)


def response_kernel(entering, rows, data, high_out, low_out, base_out):
    entering = [entering[j] for j in range(4)]
    for i in range(FAN):
        span = slice(BS * i, BS * (i + 1))
        s = own_piece(entering, i)
        both = jnp.concatenate([s, moved_on(s)], axis=0)
        y = times(both, split(rows[:, span]))
        base_out[:, span] = data[:, span] + jnp.concatenate(
            [y[ROWS : ROWS + RHS], y[:RHS]], axis=0
        )
        gain = split(jnp.concatenate([y[RHS:ROWS], y[ROWS + RHS :]], axis=0))
        high_out[:, span] = gain[0]
        low_out[:, span] = gain[1]


def device_gain(own):
    s1, s2 = own[RHS : RHS + RANK], own[RHS + RANK :]
    return jnp.concatenate([s1, s2, moved_on(s1), moved_on(s2)], axis=0)


def plane_kernel(*refs):
    *pairs, wire_out, entering_out, received = refs
    chip, core, _ = place()
    for far, pair in enumerate(pairs):
        at = 2 * lax.rem(chip + 4 - far, 4)
        received[at + core] = pair[0]
        received[at + 1 - core] = pair[1]
    entering, packed = joined(unpack(received[...]), True, True)
    wire = to_wire(packed)
    for e in range(FAN):
        wire_out[e] = wire
    for k, e in enumerate(entering):
        entering_out[k, : e.shape[0]] = e
        if e.shape[0] < ROWS:
            entering_out[k, e.shape[0] :] = jnp.zeros((ROWS - e.shape[0], WIDE), f32)


def outputs_kernel(received, own, high, low, base, first_out, second_out):
    chip, core, at = place()
    own = own_piece([own[k] for k in range(4)], 2 * chip + core)
    gain = split(device_gain(own))
    entering, _ = joined(unpack(received[...]), False, True)
    plane = own_piece(entering, at)
    state = own[:RHS] + times(plane, gain)
    both = jnp.concatenate([moved_on(state), state], axis=0)
    y = base[...] + times(both, (high[...], low[...]))
    first_out[...] = y[:RHS]
    second_out[...] = y[RHS:]


vmem = pl.BlockSpec(memory_space=pltpu.VMEM)
hbm = pl.BlockSpec(memory_space=pltpu.HBM)


def call(kernel, name, out, specs, args, scratch=(), mib=16):
    return pl.pallas_call(
        kernel,
        out_shape=out,
        in_specs=specs,
        out_specs=jax.tree.map(lambda _: vmem, out),
        scratch_shapes=scratch,
        compiler_params=pltpu.CompilerParams(vmem_limit_bytes=mib << 20),
        name=name,
    )(*args)


def shape(*dims, dtype=f32):
    return jax.ShapeDtypeStruct(dims, dtype)


def local(
    right_sides, lower_inverse, lower_left, lower_right, upper_inverse, upper_left, upper_right, block_ranks
):
    order = right_sides.shape[1]
    n = lax.axis_size("rows")
    across = [[p * FAN + d for p in range(n // FAN)] for d in range(FAN)]
    to_core = [(i, i ^ 1) for i in range(n)]

    def along_y(far):
        return [(i, i // FAN * FAN + (i + 2 * far) % FAN) for i in range(n)]

    turned = [
        jnp.swapaxes(w, 1, 2) for w in (lower_left, lower_right, upper_left, upper_right)
    ]
    thin = pltpu.VMEM((FAN, RANK, BS), bf16)
    square = pltpu.VMEM((FAN, BS, BS), bf16)
    wire, entering, rows, data = call(
        pieces_kernel,
        "pieces",
        (
            shape(WIRE, 128, dtype=bf16),
            shape(4, ROWS, WIDE),
            shape(4 * RANK, order),
            shape(2 * RHS, order),
        ),
        [hbm] * 8,
        [
            pltpu.with_memory_space_constraint(x, pltpu.HBM)
            for x in (
                block_ranks, right_sides, lower_inverse, *turned[:2], upper_inverse, *turned[2:]
            )
        ],
        [
            pltpu.SMEM(block_ranks.shape, jnp.int32), pltpu.VMEM((RHS, order), bf16), square, thin, thin, square, thin, thin,
            pltpu.SemaphoreType.DMA((8,)),
        ],
    )
    pair = jnp.stack([wire, lax.ppermute(wire, "rows", to_core)])
    chips = [pair] + [lax.ppermute(pair, "rows", along_y(far)) for far in (1, 2, 3)]
    high, low, base = call(
        response_kernel,
        "response",
        (shape(4 * RANK, order, dtype=bf16), shape(4 * RANK, order, dtype=bf16), shape(2 * RHS, order)),
        [vmem] * 3,
        (entering, rows, data),
    )
    chips[2], high, low, base = lax.optimization_barrier((chips[2], high, low, base))
    wire, own = call(
        plane_kernel,
        "plane",
        (shape(FAN, WIRE, 128, dtype=bf16), shape(4, ROWS, WIDE)),
        [vmem] * 4,
        chips,
        [pltpu.VMEM((FAN, WIRE, 128), bf16)],
    )
    received = lax.all_to_all(wire, "rows", 0, 0, tiled=True, axis_index_groups=across)
    return call(
        outputs_kernel,
        "outputs",
        (shape(RHS, order), shape(RHS, order)),
        [vmem] * 5,
        (received, own, high, low, base),
    )


def solution(mesh):
    placed_in = (
        P("rhs", "rows"),
        P("rows", None, None),
        P("rows", None, None),
        P("rows", None, None),
        P("rows", None, None),
        P("rows", None, None),
        P("rows", None, None),
        P(None, "rows"),
    )
    return jax.shard_map(
        local,
        mesh=mesh,
        in_specs=placed_in,
        out_specs=(P("rhs", "rows"), P("rhs", "rows")),
        check_vma=False,
    )
```
